512 devices in a mesh: dp: 16 (over y, x), context: 32 (over z, core).
Axes of the slice: x: 4, y: 4, z: 16, core: 2. Of those that a mesh axis runs over, the one named last changes fastest.
Arguments:
- queries: bfloat16 [131072, 2048], P(('dp', 'context')), may hold values from -6 to 6
- keys: bfloat16 [32768, 512], P(('dp', 'context')), may hold values from -6 to 6
- values: bfloat16 [32768, 512], P(('dp', 'context')), may hold values from -6 to 6
- grad_out: bfloat16 [131072, 2048], P(('dp', 'context')), may hold values from -6 to 6
- layout: int32 [16, 128, 4], replicated, may hold values from 0 to 31, as said below
- counts: int32 [16], replicated, may hold values from 1 to 4, as said below
Outputs:
- attended: bfloat16 [131072, 2048], P(('dp', 'context'))
- query_gradient: bfloat16 [131072, 2048], P(('dp', 'context'))
- key_gradient: bfloat16 [32768, 512], P(('dp', 'context'))
- value_gradient: bfloat16 [32768, 512], P(('dp', 'context'))
The draws below stay inside these ranges and needn't reach their ends.
Inputs may be any that keep to these rules, and one draw needn't show every extreme that they name: layout[h, b] lists 4 different key blocks of the sequence for query block b of head h, of which the first counts[h] are attended. Every query block of head h attends counts[h] key blocks; some head attends 4.
All inputs are finite; a program needn't handle non-finite values.
Results may differ from the reference program's by a relative error of at most 0.019.
Values may be sent and summed in bfloat16 or wider, within the bound.
A program may use at most 64 MiB of HBM per device.

```python
import math
import jax
import jax.numpy as jnp
from jax import lax

QUERY_HEADS = 16
KEY_VALUE_HEADS = 4
HEAD_WIDTH = 128
LAYOUT_BLOCK = 128
MAX_PICKED = 4
SEQUENCE_COUNT = 8
QUERY_LENGTH = 16384
KEY_LENGTH = 4096
QUERY_BLOCK_COUNT = 128


def layout_tables(key):
    base = jax.random.fold_in(key, 7101)
    key_blocks = KEY_LENGTH // LAYOUT_BLOCK
    query_blocks = QUERY_LENGTH // LAYOUT_BLOCK
    noise = jax.random.randint(jax.random.fold_in(base, 1), (QUERY_HEADS, query_blocks, key_blocks), 0, 1 << 20)
    ranked = noise * key_blocks + jnp.arange(key_blocks, dtype=jnp.int32)
    chosen = jnp.argsort(ranked, axis=-1)[:, :, :MAX_PICKED].astype(jnp.int32)
    used = jax.random.randint(jax.random.fold_in(base, 2), (QUERY_HEADS,), 1, MAX_PICKED + 1)
    busiest = jax.random.randint(jax.random.fold_in(base, 3), (), 0, QUERY_HEADS)
    used = jnp.where(jnp.arange(QUERY_HEADS) == busiest, MAX_PICKED, used).astype(jnp.int32)
    return (chosen, used)


def key_block_index(key):
    base = jax.random.fold_in(key, 7202)
    array_shape = (SEQUENCE_COUNT * KEY_LENGTH, KEY_VALUE_HEADS * HEAD_WIDTH)
    block_lookup = jnp.clip(jax.random.normal(base, array_shape, jnp.float32), -6.0, 6.0)
    return block_lookup


def draw_layout(key, part):
    return layout_tables(key)[0]


def draw_counts(key, part):
    return layout_tables(key)[1]


def draw_keys(key, part):
    return key_block_index(key).astype(jnp.bfloat16)


def draw_queries(key, part):
    base = jax.random.fold_in(key, 7303)
    array_shape = (SEQUENCE_COUNT * QUERY_LENGTH, QUERY_HEADS * HEAD_WIDTH)
    block_lookup = jnp.clip(jax.random.normal(base, array_shape, jnp.float32), -6.0, 6.0)
    return block_lookup.astype(jnp.bfloat16)


def steps_of(stream_key, dims, cuts, least, high):
    level, own = 1.0, jax.random.fold_in(stream_key, 6)
    for axis_at, shards_of in cuts:
        steps = jnp.exp(jax.random.uniform(jax.random.fold_in(own, axis_at), (shards_of,), jnp.float32, least / len(cuts), high / len(cuts)))
        level = level * jnp.repeat(steps, dims[axis_at] // shards_of).reshape([-1 if axis == axis_at else 1 for axis in range(len(dims))])
    return level


def bell_draw(own_key, extent, spread, reach, cuts=(), kind=jnp.bfloat16):
    array = jax.random.normal(own_key, extent, jnp.float32) * spread
    if len(cuts) > 0:
        array = steps_of(own_key, extent, cuts, -0.22, 0.18) * array
    return jnp.clip(array, min=-reach, max=reach).astype(kind)


def setup_inputs(seed: int = 0) -> dict:
    streams_of = jax.random.split(jax.random.key(seed), 7)
    return {
        "queries": draw_queries(jax.random.fold_in(streams_of[6], 71), 0),
        "keys": draw_keys(jax.random.fold_in(streams_of[6], 71), 0),
        "values": bell_draw(streams_of[2], (SEQUENCE_COUNT * KEY_LENGTH, KEY_VALUE_HEADS * HEAD_WIDTH), 1.0, 6.0, ((0, 512),)),
        "grad_out": bell_draw(streams_of[3], (SEQUENCE_COUNT * QUERY_LENGTH, QUERY_HEADS * HEAD_WIDTH), 1.0, 6.0, ((0, 512),)),
        "layout": draw_layout(jax.random.fold_in(streams_of[6], 71), 0),
        "counts": draw_counts(jax.random.fold_in(streams_of[6], 71), 0),
    }


def settle(tensor):
    return lax.optimization_barrier(tensor.astype(jnp.bfloat16)).astype(jnp.float32)

def one_head(query_head, grad_head, key_head, value_head, picked, head_count):
    softmax_scale = 1.0 / math.sqrt(HEAD_WIDTH)
    key_blocks = KEY_LENGTH // LAYOUT_BLOCK
    query_pieces = query_head.astype(jnp.float32).reshape(QUERY_BLOCK_COUNT, LAYOUT_BLOCK, HEAD_WIDTH)
    gradient_pieces = grad_head.astype(jnp.float32).reshape(QUERY_BLOCK_COUNT, LAYOUT_BLOCK, HEAD_WIDTH)
    key_tiles = key_head.astype(jnp.float32).reshape(key_blocks, LAYOUT_BLOCK, HEAD_WIDTH)
    value_tiles = value_head.astype(jnp.float32).reshape(key_blocks, LAYOUT_BLOCK, HEAD_WIDTH)
    key_selected = jnp.take(key_tiles, picked, axis=0)
    value_selected = jnp.take(value_tiles, picked, axis=0)
    usable = (jnp.arange(MAX_PICKED, dtype=jnp.int32) < head_count)[None, None, :, None]
    score_matrix = jnp.einsum('upv,unev->upne', query_pieces, key_selected) * softmax_scale
    score_matrix = jnp.where(usable, score_matrix, -jnp.inf)
    row_max = lax.optimization_barrier(jnp.max(score_matrix, axis=(2, 3), keepdims=True))
    log_total = row_max + jnp.log(lax.optimization_barrier(jnp.sum(jnp.exp(score_matrix - row_max), axis=(2, 3), keepdims=True)))
    weights = jnp.exp(score_matrix - log_total)
    rounded_value = settle(weights)
    attended = jnp.einsum('phos,posw->phw', rounded_value, value_selected).astype(jnp.bfloat16)
    row_delta = lax.optimization_barrier(jnp.sum(gradient_pieces * attended.astype(jnp.float32), axis=-1))[:, :, None, None]
    weight_gradient = jnp.einsum('upv,unev->upne', gradient_pieces, value_selected)
    score_gradient = settle(weights * (weight_gradient - row_delta) * softmax_scale)
    query_gradient = jnp.einsum('phos,posw->phw', score_gradient, key_selected).astype(jnp.bfloat16)
    key_portions = jnp.einsum('yoif,yov->yifv', score_gradient, query_pieces).reshape(QUERY_BLOCK_COUNT * MAX_PICKED, LAYOUT_BLOCK, HEAD_WIDTH)
    value_portions = jnp.einsum('yoif,yov->yifv', rounded_value, gradient_pieces).reshape(QUERY_BLOCK_COUNT * MAX_PICKED, LAYOUT_BLOCK, HEAD_WIDTH)
    flat_blocks = picked.reshape(-1).astype(jnp.int32)
    key_gradient = jax.ops.segment_sum(key_portions, flat_blocks, num_segments=key_blocks)
    value_gradient = jax.ops.segment_sum(value_portions, flat_blocks, num_segments=key_blocks)
    return (attended.reshape(QUERY_LENGTH, HEAD_WIDTH), query_gradient.reshape(QUERY_LENGTH, HEAD_WIDTH), key_gradient.reshape(KEY_LENGTH, HEAD_WIDTH), value_gradient.reshape(KEY_LENGTH, HEAD_WIDTH))

def reference(queries, keys, values, grad_out, layout, counts):
    group_width = QUERY_HEADS // KEY_VALUE_HEADS

    def one_sequence(sequence_index):
        query_seq = lax.dynamic_slice_in_dim(queries, sequence_index * QUERY_LENGTH, QUERY_LENGTH, 0).reshape(QUERY_LENGTH, QUERY_HEADS, HEAD_WIDTH).transpose(1, 0, 2)
        grad_seq = lax.dynamic_slice_in_dim(grad_out, sequence_index * QUERY_LENGTH, QUERY_LENGTH, 0).reshape(QUERY_LENGTH, QUERY_HEADS, HEAD_WIDTH).transpose(1, 0, 2)
        key_sequence = lax.dynamic_slice_in_dim(keys, sequence_index * KEY_LENGTH, KEY_LENGTH, 0).reshape(KEY_LENGTH, KEY_VALUE_HEADS, HEAD_WIDTH).transpose(1, 0, 2)
        value_sequence = lax.dynamic_slice_in_dim(values, sequence_index * KEY_LENGTH, KEY_LENGTH, 0).reshape(KEY_LENGTH, KEY_VALUE_HEADS, HEAD_WIDTH).transpose(1, 0, 2)

        def per_head(head_index):
            kv_index = head_index // group_width
            return one_head(query_seq[head_index], grad_seq[head_index], key_sequence[kv_index], value_sequence[kv_index], layout[head_index], counts[head_index])
        output_rows = lax.map(per_head, jnp.arange(QUERY_HEADS, dtype=jnp.int32))
        attended = output_rows[0].transpose(1, 0, 2).reshape(QUERY_LENGTH, QUERY_HEADS * HEAD_WIDTH)
        query_gradient = output_rows[1].transpose(1, 0, 2).reshape(QUERY_LENGTH, QUERY_HEADS * HEAD_WIDTH)
        key_gradient = output_rows[2].reshape(KEY_VALUE_HEADS, group_width, KEY_LENGTH, HEAD_WIDTH).sum(axis=1).astype(jnp.bfloat16)
        value_gradient = output_rows[3].reshape(KEY_VALUE_HEADS, group_width, KEY_LENGTH, HEAD_WIDTH).sum(axis=1).astype(jnp.bfloat16)
        key_gradient = key_gradient.transpose(1, 0, 2).reshape(KEY_LENGTH, KEY_VALUE_HEADS * HEAD_WIDTH)
        value_gradient = value_gradient.transpose(1, 0, 2).reshape(KEY_LENGTH, KEY_VALUE_HEADS * HEAD_WIDTH)
        return (attended, query_gradient, key_gradient, value_gradient)
    result_list = lax.map(one_sequence, jnp.arange(SEQUENCE_COUNT, dtype=jnp.int32))
    return (result_list[0].reshape(SEQUENCE_COUNT * QUERY_LENGTH, QUERY_HEADS * HEAD_WIDTH), result_list[1].reshape(SEQUENCE_COUNT * QUERY_LENGTH, QUERY_HEADS * HEAD_WIDTH), result_list[2].reshape(SEQUENCE_COUNT * KEY_LENGTH, KEY_VALUE_HEADS * HEAD_WIDTH), result_list[3].reshape(SEQUENCE_COUNT * KEY_LENGTH, KEY_VALUE_HEADS * HEAD_WIDTH))
```

```python
import functools
import math

import jax
import jax.numpy as jnp
from jax import lax
from jax.experimental import pallas as pl
from jax.experimental.pallas import tpu as pltpu
from jax.sharding import PartitionSpec as P

QUERY_HEADS = 16
KEY_VALUE_HEADS = 4
HEAD_WIDTH = 128
BLOCK = 128
GROUP_WIDTH = 4 * HEAD_WIDTH
MESH = pl.DeviceIdType.MESH
VMEM_SPEC = pl.BlockSpec(memory_space=pltpu.VMEM)
ANY_SPEC = pl.BlockSpec(memory_space=pl.ANY)
SCALE = 1.0 / math.sqrt(HEAD_WIDTH)
SCALE_LOG2E = SCALE / math.log(2.0)
ROUTES = ((0, 0), (0, 1), (1, 0), (1, 1))


class Place:
    def __init__(self, ring):
        dp = lax.axis_index("dp")
        context = lax.axis_index("context")
        self.ring = ring
        self.dp = dp
        self.member = dp % 2
        self.core = context % 2
        self.z = context // 2
        self.head = self.member * 2 + self.core

    def partner(self, route):
        flip_member, flip_core = route
        member = 1 - self.member if flip_member else self.member
        core = 1 - self.core if flip_core else self.core
        return member, core, member * 2 + core, (self.dp - self.member + member, self.z * 2 + core)

    def ring_device(self, step):
        return (self.dp, (self.z + step + self.ring) % self.ring * 2 + self.core)

    def enter(self):
        barrier = pltpu.get_barrier_semaphore()
        others = [self.partner(route)[3] for route in ROUTES[1:]]
        others += [self.ring_device(1), self.ring_device(-1)]
        for other in others:
            pl.semaphore_signal(barrier, inc=1, device_id=other, device_id_type=MESH)
        pl.semaphore_wait(barrier, len(others))


def columns(index, width):
    return pl.ds(pl.multiple_of(index * width, width), width)


def gather_kernel(
    ring, q, g, k, v, qg, gg, kf, vf, own_sem, send_x, recv_x, send_z, recv_z
):
    place = Place(ring)
    place.enter()
    half = k.shape[0]
    own_block = place.member * ring + place.z
    small, large = [], []
    for t, (source, target) in enumerate(((k, kf), (v, vf), (q, qg), (g, gg))):
        copies = small if t < 2 else large
        width = HEAD_WIDTH if t < 2 else GROUP_WIDTH
        if t < 2:
            landing = target.at[own_block, columns(place.core, half), :]
        else:
            landing = target.at[place.head]
        for i, route in enumerate(ROUTES):
            _, _, head, device = place.partner(route)
            piece = source.at[:, columns(head, width)]
            if i == 0:
                copy = pltpu.make_async_copy(piece, landing, own_sem.at[t])
            else:
                copy = pltpu.make_async_remote_copy(
                    src_ref=piece,
                    dst_ref=landing,
                    send_sem=send_x.at[t, i - 1],
                    recv_sem=recv_x.at[t, i - 1],
                    device_id=device,
                    device_id_type=MESH,
                )
            copies.append((i, copy))
            copy.start()
    for i, copy in small:
        copy.wait() if i == 0 else copy.wait_recv()

    def hop(way, chunk, slot, sub):
        buffer = (kf, vf)[sub // 2]
        sign = 1 if way == 0 else -1
        block = sub % 2 * ring + (place.z - sign * chunk + ring) % ring
        return pltpu.make_async_remote_copy(
            src_ref=buffer.at[block],
            dst_ref=buffer.at[block],
            send_sem=send_z.at[way, slot, sub],
            recv_sem=recv_z.at[way, slot, sub],
            device_id=place.ring_device(sign),
            device_id_type=MESH,
        )

    pairs = [(way, sub) for sub in range(4) for way in range(2)]
    last = [(0, 0), (1, 2), (0, 1), (1, 3)]
    far = ring // 2
    for way, sub in pairs:
        hop(way, 0, 0, sub).start()

    def forward(step, carry):
        for way, sub in pairs:
            hop(way, step, step - 1, sub).wait_recv()
            hop(way, step, step, sub).start()
        return carry

    lax.fori_loop(1, far - 1, forward, 0)
    for way, sub in pairs:
        hop(way, far - 1, far - 2, sub).wait_recv()
        if (way, sub) in last:
            hop(way, far - 1, far - 1, sub).start()
    for way, sub in last:
        hop(way, far, far - 1, sub).wait_recv()

    def drain(step, carry):
        for way, sub in pairs:
            hop(way, step, step, sub).wait_send()
        return carry

    lax.fori_loop(0, far - 1, drain, 0)
    for way, sub in last:
        hop(way, far - 1, far - 1, sub).wait_send()
    for i, copy in small:
        if i > 0:
            copy.wait_send()
    for i, copy in large:
        copy.wait()


def scatter_kernel(
    ring, o, dq, dk, dv, att, dqo, dko, dvo, landed, final, own_sem, send_x, recv_x, send_z, recv_z
):
    place = Place(ring)
    place.enter()
    half = dko.shape[0]
    copies = []

    def exchange(t, source, target, width):
        for i, route in enumerate(ROUTES):
            member, core, head, device = place.partner(route)
            piece = source(member, core, head)
            landing = target.at[:, columns(place.head, width)]
            if i == 0:
                copy = pltpu.make_async_copy(piece, landing, own_sem.at[t])
            else:
                copy = pltpu.make_async_remote_copy(
                    src_ref=piece,
                    dst_ref=landing,
                    send_sem=send_x.at[t, i - 1],
                    recv_sem=recv_x.at[t, i - 1],
                    device_id=device,
                    device_id_type=MESH,
                )
            copies.append(copy)
            copy.start()

    far = ring // 2

    def partial(sub, way, distance):
        sign = 1 if way == 0 else -1
        block = sub % 2 * ring + (place.z + sign * distance + ring) % ring
        return (dk, dv)[sub // 2].at[block]

    def hop(source, way, slot, sub):
        return pltpu.make_async_remote_copy(
            src_ref=source,
            dst_ref=landed.at[way, slot, sub],
            send_sem=send_z.at[way, slot, sub],
            recv_sem=recv_z.at[way, slot, sub],
            device_id=place.ring_device(1 if way == 0 else -1),
            device_id_type=MESH,
        )

    def pass_on(way, distance, sub):
        slot = landed.at[way, distance, sub]
        hop(slot, way, distance, sub).wait_recv()
        slot[...] = (
            slot[...].astype(jnp.float32) + partial(sub, way, distance)[...].astype(jnp.float32)
        ).astype(jnp.bfloat16)
        hop(slot, way, distance - 1, sub).start()

    pairs = [(way, sub) for sub in range(4) for way in range(2)]
    longer = [(0, 0), (1, 2), (0, 1), (1, 3)]
    shorter = [pair for pair in pairs if pair not in longer]
    for way, sub in longer:
        hop(partial(sub, way, far), way, far - 1, sub).start()
    for way, sub in shorter:
        hop(partial(sub, way, far - 1), way, far - 2, sub).start()
    exchange(0, lambda member, core, head: o.at[head], att, GROUP_WIDTH)
    exchange(1, lambda member, core, head: dq.at[head], dqo, GROUP_WIDTH)
    for way, sub in longer:
        pass_on(way, far - 1, sub)

    def steps(i, carry):
        for way, sub in longer + shorter:
            pass_on(way, far - 2 - i, sub)
        return carry

    lax.fori_loop(0, far - 2, steps, 0)
    for sub in range(4):
        for way in range(2):
            hop(landed.at[way, 0, sub], way, 0, sub).wait_recv()
        total = (
            landed[0, 0, sub].astype(jnp.float32)
            + landed[1, 0, sub].astype(jnp.float32)
            + partial(sub, 0, 0)[...].astype(jnp.float32)
        )
        if sub < 2:
            total = total * SCALE
        final[sub] = total.astype(jnp.bfloat16)
    exchange(2, lambda member, core, head: final.at[member, columns(core, half), :], dko, HEAD_WIDTH)
    exchange(
        3, lambda member, core, head: final.at[2 + member, columns(core, half), :], dvo, HEAD_WIDTH
    )

    def drain(step, carry):
        for way, sub in pairs:
            hop(landed.at[way, step, sub], way, step, sub).wait_send()
        return carry

    lax.fori_loop(0, far - 1, drain, 0)
    for way, sub in longer:
        hop(landed.at[way, far - 1, sub], way, far - 1, sub).wait_send()
    for copy in copies:
        copy.wait()


def attend(count, unroll, z_blocks, head, start, q, g, k, v, kt, vt, o, dq, dka, dva, picked):
    lanes = columns(head, HEAD_WIDTH)
    nt = (((1,), (1,)), ((), ()))
    results = []
    for u in range(unroll):
        qi = start + u
        block = qi // 4 * (z_blocks * 4) + qi % 4
        chosen = [picked(head, j, block) for j in range(count)]
        query = q[qi, :, lanes]
        grad = g[qi, :, lanes]
        scores = lax.dot_general(
            jnp.concatenate([k[b] for b in chosen], 0), query, nt, preferred_element_type=jnp.float32
        )
        dweights = lax.dot_general(
            jnp.concatenate([v[b] for b in chosen], 0), grad, nt, preferred_element_type=jnp.float32
        )
        peak = jnp.max(scores, axis=0, keepdims=True)
        powers = jnp.exp2((scores - peak) * SCALE_LOG2E)
        weights = powers * (1.0 / jnp.sum(powers, axis=0, keepdims=True))
        delta = jnp.sum(weights * dweights, axis=0, keepdims=True)
        dscores = (weights * (dweights - delta)).astype(jnp.bfloat16)
        weights = weights.astype(jnp.bfloat16)
        out = jnp.dot(
            jnp.concatenate([vt[b] for b in chosen], 1), weights, preferred_element_type=jnp.float32
        )
        o[qi, :, lanes] = out.T.astype(jnp.bfloat16)
        dquery = jnp.dot(
            jnp.concatenate([kt[b] for b in chosen], 1), dscores, preferred_element_type=jnp.float32
        )
        dq[qi, :, lanes] = (dquery.T * SCALE).astype(jnp.bfloat16)
        dkey = jnp.dot(dscores, query, preferred_element_type=jnp.float32)
        dvalue = jnp.dot(weights, grad, preferred_element_type=jnp.float32)
        results.append((chosen, dkey, dvalue))
    for chosen, dkey, dvalue in results:
        for j, b in enumerate(chosen):
            rows = slice(j * BLOCK, (j + 1) * BLOCK)
            dka[b] += dkey[rows]
            dva[b] += dvalue[rows]


def attention_kernel(
    ring, unroll, lists, counts, q, g, k, v, o, dq, dk, dv, dka, dva, kt, vt, own_lists, sem
):
    place = Place(ring)
    copy = pltpu.make_async_copy(lists.at[pl.ds(place.head * 4, 4)], own_lists, sem)
    copy.start()
    blocks = k.shape[0]

    @pl.loop(0, blocks)
    def _(b):
        kt[b] = k[b].T
        vt[b] = v[b].T
        dka[b] = jnp.zeros((BLOCK, HEAD_WIDTH), jnp.float32)
        dva[b] = jnp.zeros((BLOCK, HEAD_WIDTH), jnp.float32)

    copy.wait()

    def picked(head, j, block):
        return own_lists[head, j, place.z * 4 + block]

    @pl.loop(0, 4)
    def _(head):
        used = counts[place.head * 4 + head]
        for count in range(1, 5):

            @pl.when(used == count)
            def _():
                @pl.loop(0, 8, step=unroll)
                def _(start):
                    attend(
                        count, unroll, ring, head, start, q, g, k, v, kt, vt, o, dq, dka, dva, picked
                    )

    @pl.loop(0, blocks)
    def _(b):
        dk[b] = dka[b].astype(jnp.bfloat16)
        dv[b] = dva[b].astype(jnp.bfloat16)


def attention(ring, lists, counts, qg, gg, kf, vf, unroll=2):
    tokens = jax.ShapeDtypeStruct((8, BLOCK, GROUP_WIDTH), jnp.bfloat16)
    rows = jax.ShapeDtypeStruct(kf.shape, jnp.bfloat16)
    return pl.pallas_call(
        functools.partial(attention_kernel, ring, unroll),
        out_shape=(tokens, tokens, rows, rows),
        in_specs=[ANY_SPEC, pl.BlockSpec(memory_space=pltpu.SMEM)] + [VMEM_SPEC] * 4,
        out_specs=(VMEM_SPEC,) * 4,
        scratch_shapes=[
            pltpu.VMEM(kf.shape, jnp.float32),
            pltpu.VMEM(kf.shape, jnp.float32),
            pltpu.VMEM(kf.shape, jnp.bfloat16),
            pltpu.VMEM(kf.shape, jnp.bfloat16),
            pltpu.SMEM((4, 4, lists.shape[2]), jnp.int32),
            pltpu.SemaphoreType.DMA,
        ],
        compiler_params=pltpu.CompilerParams(vmem_limit_bytes=40 << 20),
        name="attention",
    )(lists, counts, qg, gg, kf, vf)


def link_semaphores(ring):
    return [
        pltpu.SemaphoreType.DMA((4,)),
        pltpu.SemaphoreType.DMA((4, 3)),
        pltpu.SemaphoreType.DMA((4, 3)),
        pltpu.SemaphoreType.DMA((2, ring // 2, 4)),
        pltpu.SemaphoreType.DMA((2, ring // 2, 4)),
    ]


def local(queries, keys, values, grad_out, layout, counts):
    ring = lax.axis_size("context") // 2
    tokens = jax.ShapeDtypeStruct((4, queries.shape[0], GROUP_WIDTH), jnp.bfloat16)
    rows = jax.ShapeDtypeStruct((2 * ring, BLOCK, HEAD_WIDTH), jnp.bfloat16)
    qg, gg, kf, vf = pl.pallas_call(
        functools.partial(gather_kernel, ring),
        out_shape=(tokens, tokens, rows, rows),
        in_specs=[ANY_SPEC, ANY_SPEC, VMEM_SPEC, VMEM_SPEC],
        out_specs=(VMEM_SPEC,) * 4,
        scratch_shapes=link_semaphores(ring),
        compiler_params=pltpu.CompilerParams(
            collective_id=0, has_side_effects=True, vmem_limit_bytes=24 << 20
        ),
        name="gather",
    )(queries, grad_out, keys, values)
    shape = (8, BLOCK, GROUP_WIDTH)
    o, dq, dk, dv = attention(
        ring, layout.transpose(0, 2, 1), counts, qg.reshape(shape), gg.reshape(shape), kf, vf
    )
    return pl.pallas_call(
        functools.partial(scatter_kernel, ring),
        out_shape=tuple(
            jax.ShapeDtypeStruct(x.shape, jnp.bfloat16) for x in (queries, queries, keys, values)
        ),
        in_specs=[VMEM_SPEC] * 4,
        out_specs=(ANY_SPEC,) * 4,
        scratch_shapes=[
            pltpu.VMEM((2, ring // 2, 4, BLOCK, HEAD_WIDTH), jnp.bfloat16),
            pltpu.VMEM((4, BLOCK, HEAD_WIDTH), jnp.bfloat16),
        ]
        + link_semaphores(ring),
        compiler_params=pltpu.CompilerParams(
            collective_id=1, has_side_effects=True, vmem_limit_bytes=24 << 20
        ),
        name="scatter",
    )(o.reshape(tokens.shape), dq.reshape(tokens.shape), dk, dv)


def solution(mesh):
    placed = P(("dp", "context"), None)
    return jax.shard_map(
        local,
        mesh=mesh,
        in_specs=(placed, placed, placed, placed, P(), P()),
        out_specs=(placed,) * 4,
        check_vma=False,
    )
```

```python
import functools
import math

import jax
import jax.numpy as jnp
from jax import lax
from jax.experimental import pallas as pl
from jax.experimental.pallas import tpu as pltpu
from jax.sharding import PartitionSpec as P

QUERY_HEADS = 16
KEY_VALUE_HEADS = 4
HEAD_WIDTH = 128
BLOCK = 128
GROUP_WIDTH = 4 * HEAD_WIDTH
MESH = pl.DeviceIdType.MESH
VMEM_SPEC = pl.BlockSpec(memory_space=pltpu.VMEM)
ANY_SPEC = pl.BlockSpec(memory_space=pl.ANY)
HBM_SPEC = pl.BlockSpec(memory_space=pltpu.HBM)
SCALE = 1.0 / math.sqrt(HEAD_WIDTH)
SCALE_LOG2E = SCALE / math.log(2.0)
ROUTES = ((0, 0), (0, 1), (1, 0), (1, 1))


class Place:
    def __init__(self, ring):
        dp = lax.axis_index("dp")
        context = lax.axis_index("context")
        self.ring = ring
        self.dp = dp
        self.member = dp % 2
        self.core = context % 2
        self.z = context // 2
        self.head = self.member * 2 + self.core

    def partner(self, route, step=0):
        flip_member, flip_core = route
        member = 1 - self.member if flip_member else self.member
        core = 1 - self.core if flip_core else self.core
        z = (self.z + step + self.ring) % self.ring
        return member, core, member * 2 + core, (self.dp - self.member + member, z * 2 + core)

    def greet(self):
        barrier = pltpu.get_barrier_semaphore()
        others = [
            self.partner(route, step)[3] for step in (1, -1, 0) for route in ROUTES if step or any(route)
        ]
        for other in others:
            pl.semaphore_signal(barrier, inc=1, device_id=other, device_id_type=MESH)
        return barrier, len(others)


def columns(index, width):
    return pl.ds(pl.multiple_of(index * width, width), width)


def remote(source, landing, send_sem, recv_sem, device):
    return pltpu.make_async_remote_copy(
        src_ref=source,
        dst_ref=landing,
        send_sem=send_sem,
        recv_sem=recv_sem,
        device_id=device,
        device_id_type=MESH,
    )


SIGNS = (1, -1)
PIECES = [(t, i) for i in (2, 3, 1, 0) for t in range(2)]


def gather_kernel(
    ring, q, g, k, v, qg, gg, kf, vf, kt, vt, own_sem, send_x, recv_x, send_z, recv_z
):
    place = Place(ring)
    barrier, expected = place.greet()
    pl.semaphore_wait(barrier, expected)
    half = k.shape[0]
    far = ring // 2

    def rows(buffer, route, z):
        member, core, _, _ = place.partner(route)
        return buffer.at[member * ring + z, columns(core, half), :]

    def chunk_z(way, chunk):
        return (place.z - SIGNS[way] * chunk + ring) % ring

    first, near = [], []
    for t, i in PIECES:
        piece = (k, v)[t].at[:, columns(place.partner(ROUTES[i])[2], HEAD_WIDTH)]
        landing = rows((kf, vf)[t], ROUTES[0], place.z)
        for way in range(2):
            first.append(
                remote(
                    piece,
                    landing,
                    send_z.at[way, 0, t * 4 + i],
                    recv_z.at[way, 0, t * 4 + i],
                    place.partner(ROUTES[i], SIGNS[way])[3],
                )
            )
            first[-1].start()
    for t, i in PIECES:
        piece = (k, v)[t].at[:, columns(place.partner(ROUTES[i])[2], HEAD_WIDTH)]
        landing = rows((kf, vf)[t], ROUTES[0], place.z)
        if i == 0:
            copy = pltpu.make_async_copy(piece, landing, own_sem.at[t])
        else:
            copy = remote(
                piece,
                landing,
                send_x.at[t, i - 1],
                recv_x.at[t, i - 1],
                place.partner(ROUTES[i])[3],
            )
        near.append((i, copy))
        copy.start()
    large = []
    for t, (source, target) in enumerate(((q, qg), (g, gg))):
        for i in (2, 3, 1, 0):
            _, _, head, device = place.partner(ROUTES[i])
            piece = source.at[:, columns(head, GROUP_WIDTH)]
            landing = target.at[place.head]
            if i == 0:
                copy = pltpu.make_async_copy(piece, landing, own_sem.at[2 + t])
            else:
                copy = remote(
                    piece, landing, send_x.at[2 + t, i - 1], recv_x.at[2 + t, i - 1], device
                )
            large.append(copy)
            copy.start()

    def hop(way, chunk, slot, t, i):
        piece = rows((kf, vf)[t], ROUTES[i], chunk_z(way, chunk))
        return remote(
            piece,
            piece,
            send_z.at[way, slot, t * 4 + i],
            recv_z.at[way, slot, t * 4 + i],
            place.partner(ROUTES[0], SIGNS[way])[3],
        )

    def turn(z):
        for member in range(2):
            block = member * ring + z
            kt[block] = kf[block].T
            vt[block] = vf[block].T

    def forward(step, carry):
        for t, i in reversed(PIECES):
            for way in range(2):
                hop(way, step, step - 1, t, i).wait_recv()
                hop(way, step, step, t, i).start()
        for way in range(2):
            turn(chunk_z(way, step))
        return carry

    lax.fori_loop(1, far - 1, forward, 0)
    for t, i in reversed(PIECES):
        for way in range(2):
            hop(way, far - 1, far - 2, t, i).wait_recv()
            if i % 2 == way:
                hop(way, far - 1, far - 1, t, i).start()
    for way in range(2):
        turn(chunk_z(way, far - 1))
    for i, copy in near:
        copy.wait() if i == 0 else copy.wait_recv()
    turn(place.z)
    for t, i in reversed(PIECES):
        hop(i % 2, far, far - 1, t, i).wait_recv()
    turn(chunk_z(0, far))

    def drain(step, carry):
        for t, i in PIECES:
            for way in range(2):
                hop(way, step, step, t, i).wait_send()
        return carry

    for copy in first:
        copy.wait_send()
    lax.fori_loop(1, far - 1, drain, 0)
    for t, i in PIECES:
        hop(i % 2, far - 1, far - 1, t, i).wait_send()
    for i, copy in near:
        if i > 0:
            copy.wait_send()
    for copy in large:
        copy.wait()


def scatter_kernel(
    ring, o, dq, dk, dv, att, dqo, dko, dvo, first, own, landed, own_sem, send_x, recv_x, send_z, recv_z
):
    place = Place(ring)
    barrier, expected = place.greet()
    half = dko.shape[0]
    far = ring // 2

    def partial(way, distance, t, i):
        member, core, _, _ = place.partner(ROUTES[i])
        z = (place.z + SIGNS[way] * distance + ring) % ring
        return (dk, dv)[t][member * ring + z, columns(core, half), :]

    def longer(way, i):
        return i % 2 == way

    for t, i in PIECES:
        for way in range(2):
            distance = far if longer(way, i) else far - 1
            first[way, t * 4 + i] = partial(way, distance, t, i).astype(jnp.bfloat16)
    pl.semaphore_wait(barrier, expected)

    def hop(source, way, slot, t, i, last=False):
        return remote(
            source,
            landed.at[way, slot, t * 4 + i],
            send_z.at[way, slot, t * 4 + i],
            recv_z.at[way, slot, t * 4 + i],
            place.partner(ROUTES[i if last else 0], SIGNS[way])[3],
        )

    def pass_on(way, distance, t, i, last=False):
        slot = landed.at[way, distance, t * 4 + i]
        hop(slot, way, distance, t, i).wait_recv()
        slot[...] = (slot[...].astype(jnp.float32) + partial(way, distance, t, i)).astype(
            jnp.bfloat16
        )
        hop(slot, way, distance - 1, t, i, last).start()

    for t, i in PIECES:
        for way in range(2):
            distance = far if longer(way, i) else far - 1
            hop(first.at[way, t * 4 + i], way, distance - 1, t, i).start()
    copies = []
    for t, i in PIECES:
        piece = t * 4 + i
        own[0, piece] = partial(0, 0, t, i).astype(jnp.bfloat16)
        if i > 0:
            copies.append(
                remote(
                    own.at[0, piece],
                    own.at[1, piece],
                    send_x.at[2 + t, i - 1],
                    recv_x.at[2 + t, i - 1],
                    place.partner(ROUTES[i])[3],
                )
            )
            copies[-1].start()
    for t, (source, target) in enumerate(((o, att), (dq, dqo))):
        for i in (2, 3, 1, 0):
            _, _, head, device = place.partner(ROUTES[i])
            landing = target.at[:, columns(place.head, GROUP_WIDTH)]
            if i == 0:
                copy = pltpu.make_async_copy(source.at[head], landing, own_sem.at[t])
            else:
                copy = remote(
                    source.at[head], landing, send_x.at[t, i - 1], recv_x.at[t, i - 1], device
                )
            copies.append(copy)
            copy.start()
    for t, i in PIECES:
        pass_on(i % 2, far - 1, t, i)

    def steps(n, carry):
        for t, i in PIECES:
            for way in range(2):
                pass_on(way, far - 2 - n, t, i)
        return carry

    lax.fori_loop(0, far - 3, steps, 0)
    for t, i in PIECES:
        for way in range(2):
            pass_on(way, 1, t, i, True)
    for copy in copies[:6]:
        copy.wait_recv()
    for t, i in reversed(PIECES):
        piece = t * 4 + i
        for way in range(2):
            hop(landed.at[way, 0, piece], way, 0, t, i, True).wait_recv()
        total = landed[0, 0, piece].astype(jnp.float32) + landed[1, 0, piece].astype(jnp.float32)
        total = total + own[1 if i > 0 else 0, piece].astype(jnp.float32)
        if t == 0:
            total = total * SCALE
        (dko, dvo)[t][:, columns(place.partner(ROUTES[i])[2], HEAD_WIDTH)] = total.astype(
            jnp.bfloat16
        )

    def drain(step, carry):
        for t, i in PIECES:
            for way in range(2):
                hop(landed.at[way, step, t * 4 + i], way, step, t, i).wait_send()
        return carry

    lax.fori_loop(1, far - 1, drain, 0)
    for t, i in PIECES:
        for way in range(2):
            hop(landed.at[way, 0, t * 4 + i], way, 0, t, i, True).wait_send()
        hop(landed.at[i % 2, far - 1, t * 4 + i], i % 2, far - 1, t, i).wait_send()
    for n, copy in enumerate(copies):
        if n < 6:
            copy.wait_send()
        else:
            copy.wait()


def output_kernel(*refs):
    sources, targets, sems = refs[:4], refs[4:8], refs[8]
    copies = [
        pltpu.make_async_copy(source, target, sems.at[n])
        for n, (source, target) in enumerate(zip(sources, targets))
    ]
    for copy in copies:
        copy.start()
    for copy in copies:
        copy.wait()


def attend(count, unroll, z_blocks, head, start, q, g, k, v, kt, vt, o, dq, dka, dva, picked):
    lanes = columns(head, HEAD_WIDTH)
    nt = (((1,), (1,)), ((), ()))
    results = []
    for u in range(unroll):
        qi = start + u
        block = qi // 4 * (z_blocks * 4) + qi % 4
        chosen = [picked(head, j, block) for j in range(count)]
        query = q[qi, :, lanes]
        grad = g[qi, :, lanes]
        scores = lax.dot_general(
            jnp.concatenate([k[b] for b in chosen], 0), query, nt, preferred_element_type=jnp.float32
        )
        dweights = lax.dot_general(
            jnp.concatenate([v[b] for b in chosen], 0), grad, nt, preferred_element_type=jnp.float32
        )
        peak = jnp.max(scores, axis=0, keepdims=True)
        powers = jnp.exp2((scores - peak) * SCALE_LOG2E)
        weights = powers * (1.0 / jnp.sum(powers, axis=0, keepdims=True))
        delta = jnp.sum(weights * dweights, axis=0, keepdims=True)
        dscores = (weights * (dweights - delta)).astype(jnp.bfloat16)
        weights = weights.astype(jnp.bfloat16)
        out = jnp.dot(
            jnp.concatenate([vt[b] for b in chosen], 1), weights, preferred_element_type=jnp.float32
        )
        o[qi, :, lanes] = out.T.astype(jnp.bfloat16)
        dquery = jnp.dot(
            jnp.concatenate([kt[b] for b in chosen], 1), dscores, preferred_element_type=jnp.float32
        )
        dq[qi, :, lanes] = (dquery.T * SCALE).astype(jnp.bfloat16)
        dkey = jnp.dot(dscores, query, preferred_element_type=jnp.float32)
        dvalue = jnp.dot(weights, grad, preferred_element_type=jnp.float32)
        results.append((chosen, dkey, dvalue))
    for chosen, dkey, dvalue in results:
        for j, b in enumerate(chosen):
            rows = slice(j * BLOCK, (j + 1) * BLOCK)
            dka[b] += dkey[rows]
            dva[b] += dvalue[rows]


def attention_kernel(ring, unroll, lists, counts, q, g, k, v, kt, vt, o, dq, dk, dv, own_lists, sem):
    place = Place(ring)
    copy = pltpu.make_async_copy(lists.at[pl.ds(place.head * 4, 4)], own_lists, sem)
    copy.start()

    @pl.loop(0, k.shape[0])
    def _(b):
        dk[b] = jnp.zeros((BLOCK, HEAD_WIDTH), jnp.float32)
        dv[b] = jnp.zeros((BLOCK, HEAD_WIDTH), jnp.float32)

    copy.wait()

    def picked(head, j, block):
        return own_lists[head, j, place.z * 4 + block]

    @pl.loop(0, 4)
    def _(head):
        used = counts[place.head * 4 + head]
        for count in range(1, 5):

            @pl.when(used == count)
            def _():
                @pl.loop(0, 8, step=unroll)
                def _(start):
                    attend(
                        count, unroll, ring, head, start, q, g, k, v, kt, vt, o, dq, dk, dv, picked
                    )


def attention(ring, lists, counts, qg, gg, kf, vf, kt, vt, unroll=2):
    tokens = jax.ShapeDtypeStruct((8, BLOCK, GROUP_WIDTH), jnp.bfloat16)
    rows = jax.ShapeDtypeStruct(kf.shape, jnp.float32)
    return pl.pallas_call(
        functools.partial(attention_kernel, ring, unroll),
        out_shape=(tokens, tokens, rows, rows),
        in_specs=[ANY_SPEC, pl.BlockSpec(memory_space=pltpu.SMEM)] + [VMEM_SPEC] * 6,
        out_specs=(VMEM_SPEC,) * 4,
        scratch_shapes=[
            pltpu.SMEM((4, 4, lists.shape[2]), jnp.int32),
            pltpu.SemaphoreType.DMA,
        ],
        compiler_params=pltpu.CompilerParams(vmem_limit_bytes=32 << 20),
        name="attention",
    )(lists, counts, qg, gg, kf, vf, kt, vt)


def link_semaphores(ring):
    return [
        pltpu.SemaphoreType.DMA((4,)),
        pltpu.SemaphoreType.DMA((4, 3)),
        pltpu.SemaphoreType.DMA((4, 3)),
        pltpu.SemaphoreType.DMA((2, ring // 2, 8)),
        pltpu.SemaphoreType.DMA((2, ring // 2, 8)),
    ]


def local(queries, keys, values, grad_out, layout, counts):
    ring = lax.axis_size("context") // 2
    half = keys.shape[0]
    tokens = jax.ShapeDtypeStruct((4, queries.shape[0], GROUP_WIDTH), jnp.bfloat16)
    rows = jax.ShapeDtypeStruct((2 * ring, BLOCK, HEAD_WIDTH), jnp.bfloat16)
    outs = tuple(
        jax.ShapeDtypeStruct(x.shape, jnp.bfloat16) for x in (queries, queries, keys, values)
    )
    qg, gg, kf, vf, kt, vt = pl.pallas_call(
        functools.partial(gather_kernel, ring),
        out_shape=(tokens, tokens, rows, rows, rows, rows),
        in_specs=[HBM_SPEC] * 4,
        out_specs=(VMEM_SPEC,) * 6,
        scratch_shapes=link_semaphores(ring),
        compiler_params=pltpu.CompilerParams(
            collective_id=0, has_side_effects=True, vmem_limit_bytes=47 << 20
        ),
        name="gather",
    )(queries, grad_out, keys, values)
    shape = (8, BLOCK, GROUP_WIDTH)
    o, dq, dk, dv = attention(
        ring,
        layout.transpose(0, 2, 1),
        counts,
        qg.reshape(shape),
        gg.reshape(shape),
        kf,
        vf,
        kt,
        vt,
    )
    results = pl.pallas_call(
        functools.partial(scatter_kernel, ring),
        out_shape=outs,
        in_specs=[VMEM_SPEC] * 4,
        out_specs=(VMEM_SPEC,) * 4,
        scratch_shapes=[
            pltpu.VMEM((2, 8, half, HEAD_WIDTH), jnp.bfloat16),
            pltpu.VMEM((2, 8, half, HEAD_WIDTH), jnp.bfloat16),
            pltpu.VMEM((2, ring // 2, 8, half, HEAD_WIDTH), jnp.bfloat16),
        ]
        + link_semaphores(ring),
        compiler_params=pltpu.CompilerParams(
            collective_id=1, has_side_effects=True, vmem_limit_bytes=24 << 20
        ),
        name="scatter",
    )(o.reshape(tokens.shape), dq.reshape(tokens.shape), dk, dv)
    return pl.pallas_call(
        output_kernel,
        out_shape=outs,
        in_specs=[ANY_SPEC] * 4,
        out_specs=(HBM_SPEC,) * 4,
        scratch_shapes=[pltpu.SemaphoreType.DMA((4,))],
        compiler_params=pltpu.CompilerParams(vmem_limit_bytes=1 << 20),
        name="output",
    )(*results)


def solution(mesh):
    placed = P(("dp", "context"), None)
    return jax.shard_map(
        local,
        mesh=mesh,
        in_specs=(placed, placed, placed, placed, P(), P()),
        out_specs=(placed,) * 4,
        check_vma=False,
    )
```

```python
import functools
import math

import jax
import jax.numpy as jnp
from jax import lax
from jax.experimental import pallas as pl
from jax.experimental.pallas import tpu as pltpu
from jax.sharding import PartitionSpec as P

QUERY_HEADS = 16
KEY_VALUE_HEADS = 4
HEAD_WIDTH = 128
BLOCK = 128
GROUP_WIDTH = 4 * HEAD_WIDTH
MESH = pl.DeviceIdType.MESH
VMEM_SPEC = pl.BlockSpec(memory_space=pltpu.VMEM)
ANY_SPEC = pl.BlockSpec(memory_space=pl.ANY)
HBM_SPEC = pl.BlockSpec(memory_space=pltpu.HBM)
SCALE = 1.0 / math.sqrt(HEAD_WIDTH)
SCALE_LOG2E = SCALE / math.log(2.0)
ROUTES = ((0, 0), (0, 1), (1, 0), (1, 1))


class Place:
    def __init__(self, ring):
        dp = lax.axis_index("dp")
        context = lax.axis_index("context")
        self.ring = ring
        self.dp = dp
        self.member = dp % 2
        self.core = context % 2
        self.z = context // 2
        self.head = self.member * 2 + self.core

    def partner(self, route, step=0):
        flip_member, flip_core = route
        member = 1 - self.member if flip_member else self.member
        core = 1 - self.core if flip_core else self.core
        z = (self.z + step + self.ring) % self.ring
        return member, core, member * 2 + core, (self.dp - self.member + member, z * 2 + core)

    def greet(self):
        barrier = pltpu.get_barrier_semaphore()
        others = [
            self.partner(route, step)[3] for step in (1, -1, 0) for route in ROUTES if step or any(route)
        ]
        for other in others:
            pl.semaphore_signal(barrier, inc=1, device_id=other, device_id_type=MESH)
        return barrier, len(others)


def columns(index, width):
    return pl.ds(pl.multiple_of(index * width, width), width)


def remote(source, landing, send_sem, recv_sem, device):
    return pltpu.make_async_remote_copy(
        src_ref=source,
        dst_ref=landing,
        send_sem=send_sem,
        recv_sem=recv_sem,
        device_id=device,
        device_id_type=MESH,
    )


SIGNS = (1, -1)
PIECES = [(t, i) for i in (2, 3, 1, 0) for t in range(2)]


def gather_kernel(
    ring, q, g, k, v, qg, gg, kf, vf, kt, vt, own_sem, send_x, recv_x, send_z, recv_z
):
    place = Place(ring)
    barrier, expected = place.greet()
    pl.semaphore_wait(barrier, expected)
    half = k.shape[0]
    far = ring // 2

    def rows(buffer, route, z):
        member, core, _, _ = place.partner(route)
        return buffer.at[member * ring + z, columns(core, half), :]

    def chunk_z(way, chunk):
        return (place.z - SIGNS[way] * chunk + ring) % ring

    first, near = [], []
    for t, i in PIECES:
        piece = (k, v)[t].at[:, columns(place.partner(ROUTES[i])[2], HEAD_WIDTH)]
        landing = rows((kf, vf)[t], ROUTES[0], place.z)
        for way in range(2):
            first.append(
                remote(
                    piece,
                    landing,
                    send_z.at[way, 0, t * 4 + i],
                    recv_z.at[way, 0, t * 4 + i],
                    place.partner(ROUTES[i], SIGNS[way])[3],
                )
            )
            first[-1].start()
    for t, i in PIECES:
        piece = (k, v)[t].at[:, columns(place.partner(ROUTES[i])[2], HEAD_WIDTH)]
        landing = rows((kf, vf)[t], ROUTES[0], place.z)
        if i == 0:
            copy = pltpu.make_async_copy(piece, landing, own_sem.at[t])
        else:
            copy = remote(
                piece,
                landing,
                send_x.at[t, i - 1],
                recv_x.at[t, i - 1],
                place.partner(ROUTES[i])[3],
            )
        near.append((i, copy))
        copy.start()
    large = []
    for t, (source, target) in enumerate(((q, qg), (g, gg))):
        for i in (2, 3, 1, 0):
            _, _, head, device = place.partner(ROUTES[i])
            piece = source.at[:, columns(head, GROUP_WIDTH)]
            landing = target.at[place.head]
            if i == 0:
                copy = pltpu.make_async_copy(piece, landing, own_sem.at[2 + t])
            else:
                copy = remote(
                    piece, landing, send_x.at[2 + t, i - 1], recv_x.at[2 + t, i - 1], device
                )
            large.append(copy)
            copy.start()

    def hop(way, chunk, slot, t, i):
        piece = rows((kf, vf)[t], ROUTES[i], chunk_z(way, chunk))
        return remote(
            piece,
            piece,
            send_z.at[way, slot, t * 4 + i],
            recv_z.at[way, slot, t * 4 + i],
            place.partner(ROUTES[0], SIGNS[way])[3],
        )

    def turn(z):
        for member in range(2):
            block = member * ring + z
            kt[block] = kf[block].T
            vt[block] = vf[block].T

    def forward(step, carry):
        for t, i in reversed(PIECES):
            for way in range(2):
                hop(way, step, step - 1, t, i).wait_recv()
                hop(way, step, step, t, i).start()
        for way in range(2):
            turn(chunk_z(way, step))
        return carry

    lax.fori_loop(1, far - 1, forward, 0)
    for t, i in reversed(PIECES):
        for way in range(2):
            hop(way, far - 1, far - 2, t, i).wait_recv()
            if i % 2 == way:
                hop(way, far - 1, far - 1, t, i).start()
    for way in range(2):
        turn(chunk_z(way, far - 1))
    for i, copy in near:
        copy.wait() if i == 0 else copy.wait_recv()
    turn(place.z)
    for t, i in reversed(PIECES):
        hop(i % 2, far, far - 1, t, i).wait_recv()
    turn(chunk_z(0, far))

    def drain(step, carry):
        for t, i in PIECES:
            for way in range(2):
                hop(way, step, step, t, i).wait_send()
        return carry

    for copy in first:
        copy.wait_send()
    lax.fori_loop(1, far - 1, drain, 0)
    for t, i in PIECES:
        hop(i % 2, far - 1, far - 1, t, i).wait_send()
    for i, copy in near:
        if i > 0:
            copy.wait_send()
    for copy in large:
        copy.wait()


def scatter_kernel(
    ring,
    lists,
    wt,
    ds,
    kt,
    vt,
    dk,
    dv,
    att,
    dqo,
    dko,
    dvo,
    o,
    dq,
    first,
    own,
    landed,
    own_lists,
    list_sem,
    own_sem,
    send_x,
    recv_x,
    send_z,
    recv_z,
):
    place = Place(ring)
    barrier, expected = place.greet()
    list_copy = pltpu.make_async_copy(lists.at[pl.ds(place.head * 4, 4)], own_lists, list_sem)
    list_copy.start()
    half = dko.shape[0]
    far = ring // 2

    def partial(way, distance, t, i):
        member, core, _, _ = place.partner(ROUTES[i])
        z = (place.z + SIGNS[way] * distance + ring) % ring
        return (dk, dv)[t][member * ring + z, columns(core, half), :]

    def longer(way, i):
        return i % 2 == way

    for t, i in PIECES:
        for way in range(2):
            distance = far if longer(way, i) else far - 1
            first[way, t * 4 + i] = partial(way, distance, t, i).astype(jnp.bfloat16)
    pl.semaphore_wait(barrier, expected)

    def hop(source, way, slot, t, i, last=False):
        return remote(
            source,
            landed.at[way, slot, t * 4 + i],
            send_z.at[way, slot, t * 4 + i],
            recv_z.at[way, slot, t * 4 + i],
            place.partner(ROUTES[i if last else 0], SIGNS[way])[3],
        )

    def pass_on(way, distance, t, i, last=False):
        slot = landed.at[way, distance, t * 4 + i]
        hop(slot, way, distance, t, i).wait_recv()
        slot[...] = (slot[...].astype(jnp.float32) + partial(way, distance, t, i)).astype(
            jnp.bfloat16
        )
        hop(slot, way, distance - 1, t, i, last).start()

    for t, i in PIECES:
        for way in range(2):
            distance = far if longer(way, i) else far - 1
            hop(first.at[way, t * 4 + i], way, distance - 1, t, i).start()
    copies = []
    for t, i in PIECES:
        piece = t * 4 + i
        own[0, piece] = partial(0, 0, t, i).astype(jnp.bfloat16)
        if i > 0:
            copies.append(
                remote(
                    own.at[0, piece],
                    own.at[1, piece],
                    send_x.at[2 + t, i - 1],
                    recv_x.at[2 + t, i - 1],
                    place.partner(ROUTES[i])[3],
                )
            )
            copies[-1].start()
    def finish(i):
        _, _, slot, device = place.partner(ROUTES[i])
        for block in range(2):
            qi = slot * 2 + block
            at = place.z * 4 + qi // 4 * (ring * 4) + qi % 4
            rows = slice(block * BLOCK, (block + 1) * BLOCK)
            for head in range(4):
                lanes = slice(head * HEAD_WIDTH, (head + 1) * HEAD_WIDTH)
                chosen = [own_lists[head, j, at] for j in range(4)]
                out = jnp.dot(
                    jnp.concatenate([vt[b] for b in chosen], 1),
                    wt[qi * 4 + head],
                    preferred_element_type=jnp.float32,
                )
                o[slot, rows, lanes] = out.T.astype(jnp.bfloat16)
                out = jnp.dot(
                    jnp.concatenate([kt[b] for b in chosen], 1),
                    ds[qi * 4 + head],
                    preferred_element_type=jnp.float32,
                )
                dq[slot, rows, lanes] = (out.T * SCALE).astype(jnp.bfloat16)
        for t, (source, target) in enumerate(((o, att), (dq, dqo))):
            landing = target.at[:, columns(place.head, GROUP_WIDTH)]
            if i == 0:
                copy = pltpu.make_async_copy(source.at[slot], landing, own_sem.at[t])
            else:
                copy = remote(
                    source.at[slot], landing, send_x.at[t, i - 1], recv_x.at[t, i - 1], device
                )
            copies.append(copy)
            copy.start()

    list_copy.wait()
    finish(2)
    for t, i in PIECES:
        pass_on(i % 2, far - 1, t, i)
    finish(3)
    for distance in (far - 2, far - 3):
        for t, i in PIECES:
            for way in range(2):
                pass_on(way, distance, t, i)
        finish(far - 1 - distance if distance == far - 2 else 0)

    def steps(n, carry):
        for t, i in PIECES:
            for way in range(2):
                pass_on(way, far - 4 - n, t, i)
        return carry

    lax.fori_loop(0, far - 5, steps, 0)
    for t, i in PIECES:
        for way in range(2):
            pass_on(way, 1, t, i, True)
    for copy in copies[:6]:
        copy.wait_recv()
    for t, i in reversed(PIECES):
        piece = t * 4 + i
        for way in range(2):
            hop(landed.at[way, 0, piece], way, 0, t, i, True).wait_recv()
        total = landed[0, 0, piece].astype(jnp.float32) + landed[1, 0, piece].astype(jnp.float32)
        total = total + own[1 if i > 0 else 0, piece].astype(jnp.float32)
        if t == 0:
            total = total * SCALE
        (dko, dvo)[t][:, columns(place.partner(ROUTES[i])[2], HEAD_WIDTH)] = total.astype(
            jnp.bfloat16
        )

    def drain(step, carry):
        for t, i in PIECES:
            for way in range(2):
                hop(landed.at[way, step, t * 4 + i], way, step, t, i).wait_send()
        return carry

    lax.fori_loop(1, far - 1, drain, 0)
    for t, i in PIECES:
        for way in range(2):
            hop(landed.at[way, 0, t * 4 + i], way, 0, t, i, True).wait_send()
        hop(landed.at[i % 2, far - 1, t * 4 + i], i % 2, far - 1, t, i).wait_send()
    for n, copy in enumerate(copies):
        if n < 6:
            copy.wait_send()
        else:
            copy.wait()


def output_kernel(*refs):
    sources, targets, sems = refs[:4], refs[4:8], refs[8]
    copies = [
        pltpu.make_async_copy(source, target, sems.at[n])
        for n, (source, target) in enumerate(zip(sources, targets))
    ]
    for copy in copies:
        copy.start()
    for copy in copies:
        copy.wait()


def attend(count, unroll, z_blocks, head, start, q, g, k, v, wt, ds, dk, dv, picked):
    lanes = columns(head, HEAD_WIDTH)
    nt = (((1,), (1,)), ((), ()))
    results = []
    for u in range(unroll):
        qi = start + u
        block = qi // 4 * (z_blocks * 4) + qi % 4
        chosen = [picked(head, j, block) for j in range(count)]
        query = q[qi, :, lanes]
        grad = g[qi, :, lanes]
        scores = lax.dot_general(
            jnp.concatenate([k[b] for b in chosen], 0), query, nt, preferred_element_type=jnp.float32
        )
        dweights = lax.dot_general(
            jnp.concatenate([v[b] for b in chosen], 0), grad, nt, preferred_element_type=jnp.float32
        )
        peak = jnp.max(scores, axis=0, keepdims=True)
        powers = jnp.exp2((scores - peak) * SCALE_LOG2E)
        weights = powers * (1.0 / jnp.sum(powers, axis=0, keepdims=True))
        delta = jnp.sum(weights * dweights, axis=0, keepdims=True)
        dscores = (weights * (dweights - delta)).astype(jnp.bfloat16)
        weights = weights.astype(jnp.bfloat16)
        item = qi * 4 + head
        wt[item, : count * BLOCK] = weights
        ds[item, : count * BLOCK] = dscores
        if count < 4:
            rest = jnp.zeros(((4 - count) * BLOCK, BLOCK), jnp.bfloat16)
            wt[item, count * BLOCK :] = rest
            ds[item, count * BLOCK :] = rest
        dkey = jnp.dot(dscores, query, preferred_element_type=jnp.float32)
        dvalue = jnp.dot(weights, grad, preferred_element_type=jnp.float32)
        results.append((chosen, dkey, dvalue))
    for chosen, dkey, dvalue in results:
        for j, b in enumerate(chosen):
            rows = slice(j * BLOCK, (j + 1) * BLOCK)
            dk[b] += dkey[rows]
            dv[b] += dvalue[rows]


def attention_kernel(ring, unroll, lists, counts, q, g, k, v, wt, ds, dk, dv, own_lists, sem):
    place = Place(ring)
    copy = pltpu.make_async_copy(lists.at[pl.ds(place.head * 4, 4)], own_lists, sem)
    copy.start()

    @pl.loop(0, k.shape[0])
    def _(b):
        dk[b] = jnp.zeros((BLOCK, HEAD_WIDTH), jnp.float32)
        dv[b] = jnp.zeros((BLOCK, HEAD_WIDTH), jnp.float32)

    copy.wait()

    def picked(head, j, block):
        return own_lists[head, j, place.z * 4 + block]

    @pl.loop(0, 4)
    def _(head):
        used = counts[place.head * 4 + head]
        for count in range(1, 5):

            @pl.when(used == count)
            def _():
                @pl.loop(0, 8, step=unroll)
                def _(start):
                    attend(count, unroll, ring, head, start, q, g, k, v, wt, ds, dk, dv, picked)


def attention(ring, lists, counts, qg, gg, kf, vf, unroll=2):
    items = jax.ShapeDtypeStruct((32, 4 * BLOCK, BLOCK), jnp.bfloat16)
    rows = jax.ShapeDtypeStruct(kf.shape, jnp.float32)
    return pl.pallas_call(
        functools.partial(attention_kernel, ring, unroll),
        out_shape=(items, items, rows, rows),
        in_specs=[ANY_SPEC, pl.BlockSpec(memory_space=pltpu.SMEM)] + [VMEM_SPEC] * 4,
        out_specs=(VMEM_SPEC,) * 4,
        scratch_shapes=[
            pltpu.SMEM((4, 4, lists.shape[2]), jnp.int32),
            pltpu.SemaphoreType.DMA,
        ],
        compiler_params=pltpu.CompilerParams(vmem_limit_bytes=32 << 20),
        name="attention",
    )(lists, counts, qg, gg, kf, vf)


def link_semaphores(ring):
    return [
        pltpu.SemaphoreType.DMA((4,)),
        pltpu.SemaphoreType.DMA((4, 3)),
        pltpu.SemaphoreType.DMA((4, 3)),
        pltpu.SemaphoreType.DMA((2, ring // 2, 8)),
        pltpu.SemaphoreType.DMA((2, ring // 2, 8)),
    ]


def local(queries, keys, values, grad_out, layout, counts):
    ring = lax.axis_size("context") // 2
    half = keys.shape[0]
    tokens = jax.ShapeDtypeStruct((4, queries.shape[0], GROUP_WIDTH), jnp.bfloat16)
    rows = jax.ShapeDtypeStruct((2 * ring, BLOCK, HEAD_WIDTH), jnp.bfloat16)
    outs = tuple(
        jax.ShapeDtypeStruct(x.shape, jnp.bfloat16) for x in (queries, queries, keys, values)
    )
    qg, gg, kf, vf, kt, vt = pl.pallas_call(
        functools.partial(gather_kernel, ring),
        out_shape=(tokens, tokens, rows, rows, rows, rows),
        in_specs=[HBM_SPEC] * 4,
        out_specs=(VMEM_SPEC,) * 6,
        scratch_shapes=link_semaphores(ring),
        compiler_params=pltpu.CompilerParams(
            collective_id=0, has_side_effects=True, vmem_limit_bytes=47 << 20
        ),
        name="gather",
    )(queries, grad_out, keys, values)
    shape = (8, BLOCK, GROUP_WIDTH)
    lists = layout.transpose(0, 2, 1)
    wt, ds, dk, dv = attention(ring, lists, counts, qg.reshape(shape), gg.reshape(shape), kf, vf)
    results = pl.pallas_call(
        functools.partial(scatter_kernel, ring),
        out_shape=outs,
        in_specs=[ANY_SPEC] + [VMEM_SPEC] * 6,
        out_specs=(VMEM_SPEC,) * 4,
        scratch_shapes=[
            pltpu.VMEM(tokens.shape, jnp.bfloat16),
            pltpu.VMEM(tokens.shape, jnp.bfloat16),
            pltpu.VMEM((2, 8, half, HEAD_WIDTH), jnp.bfloat16),
            pltpu.VMEM((2, 8, half, HEAD_WIDTH), jnp.bfloat16),
            pltpu.VMEM((2, ring // 2, 8, half, HEAD_WIDTH), jnp.bfloat16),
            pltpu.SMEM((4, 4, lists.shape[2]), jnp.int32),
            pltpu.SemaphoreType.DMA,
        ]
        + link_semaphores(ring),
        compiler_params=pltpu.CompilerParams(
            collective_id=1, has_side_effects=True, vmem_limit_bytes=24 << 20
        ),
        name="scatter",
    )(lists, wt, ds, kt, vt, dk, dv)
    return pl.pallas_call(
        output_kernel,
        out_shape=outs,
        in_specs=[ANY_SPEC] * 4,
        out_specs=(HBM_SPEC,) * 4,
        scratch_shapes=[pltpu.SemaphoreType.DMA((4,))],
        compiler_params=pltpu.CompilerParams(vmem_limit_bytes=1 << 20),
        name="output",
    )(*results)


def solution(mesh):
    placed = P(("dp", "context"), None)
    return jax.shard_map(
        local,
        mesh=mesh,
        in_specs=(placed, placed, placed, placed, P(), P()),
        out_specs=(placed,) * 4,
        check_vma=False,
    )
```

```python
import functools
import math

import jax
import jax.numpy as jnp
from jax import lax
from jax.experimental import pallas as pl
from jax.experimental.pallas import tpu as pltpu
from jax.sharding import PartitionSpec as P

QUERY_HEADS = 16
KEY_VALUE_HEADS = 4
HEAD_WIDTH = 128
BLOCK = 128
GROUP_WIDTH = 4 * HEAD_WIDTH
MESH = pl.DeviceIdType.MESH
VMEM_SPEC = pl.BlockSpec(memory_space=pltpu.VMEM)
ANY_SPEC = pl.BlockSpec(memory_space=pl.ANY)
HBM_SPEC = pl.BlockSpec(memory_space=pltpu.HBM)
SCALE = 1.0 / math.sqrt(HEAD_WIDTH)
SCALE_LOG2E = SCALE / math.log(2.0)
ROUTES = ((0, 0), (0, 1), (1, 0), (1, 1))


class Place:
    def __init__(self, ring):
        dp = lax.axis_index("dp")
        context = lax.axis_index("context")
        self.ring = ring
        self.dp = dp
        self.member = dp % 2
        self.core = context % 2
        self.z = context // 2
        self.head = self.member * 2 + self.core

    def partner(self, route, step=0):
        flip_member, flip_core = route
        member = 1 - self.member if flip_member else self.member
        core = 1 - self.core if flip_core else self.core
        z = (self.z + step + self.ring) % self.ring
        return member, core, member * 2 + core, (self.dp - self.member + member, z * 2 + core)

    def greet(self):
        barrier = pltpu.get_barrier_semaphore()
        others = [
            self.partner(route, step)[3] for step in (1, -1, 0) for route in ROUTES if step or any(route)
        ]
        for other in others:
            pl.semaphore_signal(barrier, inc=1, device_id=other, device_id_type=MESH)
        return barrier, len(others)


def columns(index, width):
    return pl.ds(pl.multiple_of(index * width, width), width)


def remote(source, landing, send_sem, recv_sem, device):
    return pltpu.make_async_remote_copy(
        src_ref=source,
        dst_ref=landing,
        send_sem=send_sem,
        recv_sem=recv_sem,
        device_id=device,
        device_id_type=MESH,
    )


SIGNS = (1, -1)
PIECES = [(t, i) for i in (2, 3, 1, 0) for t in range(2)]


def gather_kernel(
    ring, q, g, k, v, qg, gg, kf, vf, kt, vt, own_sem, send_x, recv_x, send_z, recv_z
):
    place = Place(ring)
    barrier, expected = place.greet()
    pl.semaphore_wait(barrier, expected)
    half = k.shape[0]
    far = ring // 2

    def rows(buffer, route, z):
        member, core, _, _ = place.partner(route)
        return buffer.at[member * ring + z, columns(core, half), :]

    def chunk_z(way, chunk):
        return (place.z - SIGNS[way] * chunk + ring) % ring

    first, near = [], []
    for t, i in PIECES:
        piece = (k, v)[t].at[:, columns(place.partner(ROUTES[i])[2], HEAD_WIDTH)]
        landing = rows((kf, vf)[t], ROUTES[0], place.z)
        for way in range(2):
            first.append(
                remote(
                    piece,
                    landing,
                    send_z.at[way, 0, t * 4 + i],
                    recv_z.at[way, 0, t * 4 + i],
                    place.partner(ROUTES[i], SIGNS[way])[3],
                )
            )
            first[-1].start()
    for t, i in PIECES:
        piece = (k, v)[t].at[:, columns(place.partner(ROUTES[i])[2], HEAD_WIDTH)]
        landing = rows((kf, vf)[t], ROUTES[0], place.z)
        if i == 0:
            copy = pltpu.make_async_copy(piece, landing, own_sem.at[t])
        else:
            copy = remote(
                piece,
                landing,
                send_x.at[t, i - 1],
                recv_x.at[t, i - 1],
                place.partner(ROUTES[i])[3],
            )
        near.append((i, copy))
        copy.start()
    large = []
    for t, (source, target) in enumerate(((q, qg), (g, gg))):
        for i in (2, 3, 1, 0):
            _, _, head, device = place.partner(ROUTES[i])
            piece = source.at[:, columns(head, GROUP_WIDTH)]
            landing = target.at[place.head]
            if i == 0:
                copy = pltpu.make_async_copy(piece, landing, own_sem.at[2 + t])
            else:
                copy = remote(
                    piece, landing, send_x.at[2 + t, i - 1], recv_x.at[2 + t, i - 1], device
                )
            large.append(copy)
            copy.start()

    def hop(way, chunk, slot, t, i):
        piece = rows((kf, vf)[t], ROUTES[i], chunk_z(way, chunk))
        return remote(
            piece,
            piece,
            send_z.at[way, slot, t * 4 + i],
            recv_z.at[way, slot, t * 4 + i],
            place.partner(ROUTES[0], SIGNS[way])[3],
        )

    def turn(z):
        for member in range(2):
            block = member * ring + z
            kt[block] = kf[block].T
            vt[block] = vf[block].T

    def forward(step, carry):
        for t, i in reversed(PIECES):
            for way in range(2):
                hop(way, step, step - 1, t, i).wait_recv()
                hop(way, step, step, t, i).start()
        for way in range(2):
            turn(chunk_z(way, step))
        return carry

    lax.fori_loop(1, far - 1, forward, 0)
    for t, i in reversed(PIECES):
        for way in range(2):
            hop(way, far - 1, far - 2, t, i).wait_recv()
            if i % 2 == way:
                hop(way, far - 1, far - 1, t, i).start()
    for way in range(2):
        turn(chunk_z(way, far - 1))
    for i, copy in near:
        copy.wait() if i == 0 else copy.wait_recv()
    turn(place.z)
    for t, i in reversed(PIECES):
        hop(i % 2, far, far - 1, t, i).wait_recv()
    turn(chunk_z(0, far))

    def drain(step, carry):
        for t, i in PIECES:
            for way in range(2):
                hop(way, step, step, t, i).wait_send()
        return carry

    for copy in first:
        copy.wait_send()
    lax.fori_loop(1, far - 1, drain, 0)
    for t, i in PIECES:
        hop(i % 2, far - 1, far - 1, t, i).wait_send()
    for i, copy in near:
        if i > 0:
            copy.wait_send()
    for copy in large:
        copy.wait()


def scatter_kernel(
    ring,
    lists,
    wt,
    ds,
    kt,
    vt,
    dk,
    dv,
    att,
    dqo,
    dko,
    dvo,
    o,
    dq,
    first,
    own,
    landed,
    own_lists,
    list_sem,
    own_sem,
    send_x,
    recv_x,
    send_z,
    recv_z,
):
    place = Place(ring)
    barrier, expected = place.greet()
    list_copy = pltpu.make_async_copy(lists.at[pl.ds(place.head * 4, 4)], own_lists, list_sem)
    list_copy.start()
    half = dko.shape[0]
    far = ring // 2

    def partial(way, distance, t, i):
        member, core, _, _ = place.partner(ROUTES[i])
        z = (place.z + SIGNS[way] * distance + ring) % ring
        return (dk, dv)[t][member * ring + z, columns(core, half), :]

    def longer(way, i):
        return i % 2 == way

    for t, i in PIECES:
        for way in range(2):
            distance = far if longer(way, i) else far - 1
            first[way, t * 4 + i] = partial(way, distance, t, i).astype(jnp.bfloat16)
    pl.semaphore_wait(barrier, expected)

    def hop(source, way, slot, t, i, last=False):
        return remote(
            source,
            landed.at[way, slot, t * 4 + i],
            send_z.at[way, slot, t * 4 + i],
            recv_z.at[way, slot, t * 4 + i],
            place.partner(ROUTES[i if last else 0], SIGNS[way])[3],
        )

    def pass_on(way, distance, t, i, last=False):
        slot = landed.at[way, distance, t * 4 + i]
        hop(slot, way, distance, t, i).wait_recv()
        slot[...] = (slot[...].astype(jnp.float32) + partial(way, distance, t, i)).astype(
            jnp.bfloat16
        )
        hop(slot, way, distance - 1, t, i, last).start()

    for t, i in PIECES:
        for way in range(2):
            distance = far if longer(way, i) else far - 1
            hop(first.at[way, t * 4 + i], way, distance - 1, t, i).start()
    copies = []
    for t, i in PIECES:
        piece = t * 4 + i
        own[0, piece] = partial(0, 0, t, i).astype(jnp.bfloat16)
        if i > 0:
            copies.append(
                remote(
                    own.at[0, piece],
                    own.at[1, piece],
                    send_x.at[2 + t, i - 1],
                    recv_x.at[2 + t, i - 1],
                    place.partner(ROUTES[i])[3],
                )
            )
            copies[-1].start()
    def finish(i):
        _, _, slot, device = place.partner(ROUTES[i])
        for block in range(2):
            qi = slot * 2 + block
            at = place.z * 4 + qi // 4 * (ring * 4) + qi % 4
            rows = slice(block * BLOCK, (block + 1) * BLOCK)
            for head in range(4):
                lanes = slice(head * HEAD_WIDTH, (head + 1) * HEAD_WIDTH)
                chosen = [own_lists[head, j, at] for j in range(4)]
                out = jnp.dot(
                    jnp.concatenate([vt[b] for b in chosen], 1),
                    wt[qi * 4 + head],
                    preferred_element_type=jnp.float32,
                )
                o[slot, rows, lanes] = out.T.astype(jnp.bfloat16)
                out = jnp.dot(
                    jnp.concatenate([kt[b] for b in chosen], 1),
                    ds[qi * 4 + head],
                    preferred_element_type=jnp.float32,
                )
                dq[slot, rows, lanes] = (out.T * SCALE).astype(jnp.bfloat16)
        for t, (source, target) in enumerate(((o, att), (dq, dqo))):
            landing = target.at[:, columns(place.head, GROUP_WIDTH)]
            if i == 0:
                copy = pltpu.make_async_copy(source.at[slot], landing, own_sem.at[t])
            else:
                copy = remote(
                    source.at[slot], landing, send_x.at[t, i - 1], recv_x.at[t, i - 1], device
                )
            copies.append(copy)
            copy.start()

    list_copy.wait()
    finish(2)
    for t, i in PIECES:
        pass_on(i % 2, far - 1, t, i)
    finish(3)
    for distance in (far - 2, far - 3):
        for t, i in PIECES:
            for way in range(2):
                pass_on(way, distance, t, i)
        finish(far - 1 - distance if distance == far - 2 else 0)

    def steps(n, carry):
        for t, i in PIECES:
            for way in range(2):
                pass_on(way, far - 4 - n, t, i)
        return carry

    lax.fori_loop(0, far - 5, steps, 0)
    for t, i in PIECES:
        for way in range(2):
            pass_on(way, 1, t, i, True)
    for copy in copies[:6]:
        copy.wait_recv()
    for t, i in reversed(PIECES):
        piece = t * 4 + i
        for way in range(2):
            hop(landed.at[way, 0, piece], way, 0, t, i, True).wait_recv()
        total = landed[0, 0, piece].astype(jnp.float32) + landed[1, 0, piece].astype(jnp.float32)
        total = total + own[1 if i > 0 else 0, piece].astype(jnp.float32)
        if t == 0:
            total = total * SCALE
        (dko, dvo)[t][:, columns(place.partner(ROUTES[i])[2], HEAD_WIDTH)] = total.astype(
            jnp.bfloat16
        )

    def drain(step, carry):
        for t, i in PIECES:
            for way in range(2):
                hop(landed.at[way, step, t * 4 + i], way, step, t, i).wait_send()
        return carry

    lax.fori_loop(1, far - 1, drain, 0)
    for t, i in PIECES:
        for way in range(2):
            hop(landed.at[way, 0, t * 4 + i], way, 0, t, i, True).wait_send()
        hop(landed.at[i % 2, far - 1, t * 4 + i], i % 2, far - 1, t, i).wait_send()
    for n, copy in enumerate(copies):
        if n < 6:
            copy.wait_send()
        else:
            copy.wait()


def output_kernel(*refs):
    sources, targets, sems = refs[:4], refs[4:8], refs[8]
    copies = [
        pltpu.make_async_copy(source, target, sems.at[n])
        for n, (source, target) in enumerate(zip(sources, targets))
    ]
    for copy in copies:
        copy.start()
    for copy in copies:
        copy.wait()


def attend(count, unroll, z_blocks, head, start, q, g, k, v, wt, ds, dk, dv, picked, held):
    lanes = columns(head, HEAD_WIDTH)
    nt = (((1,), (1,)), ((), ()))
    items = []
    for u in range(unroll):
        qi = start + u
        block = qi // 4 * (z_blocks * 4) + qi % 4
        items.append((qi, [picked(head, j, block) for j in range(count)]))

    def products(n):
        qi, chosen = items[n]
        for j, b in enumerate(chosen):
            rows = slice(j * BLOCK, (j + 1) * BLOCK)
            held[n % 2, 0, rows] = lax.dot_general(
                k[b], q[qi, :, lanes], nt, preferred_element_type=jnp.float32
            )
            held[n % 2, 1, rows] = lax.dot_general(
                v[b], g[qi, :, lanes], nt, preferred_element_type=jnp.float32
            )

    def softmax(n):
        qi, chosen = items[n]
        parts = [slice(j * BLOCK, (j + 1) * BLOCK) for j in range(count)]
        peak = functools.reduce(jnp.maximum, [held[n % 2, 0, rows] for rows in parts])
        peak = jnp.max(peak, axis=0, keepdims=True)
        total = delta = 0.0
        for rows in parts:
            powers = jnp.exp2((held[n % 2, 0, rows] - peak) * SCALE_LOG2E)
            held[n % 2, 0, rows] = powers
            total = total + powers
            delta = delta + powers * held[n % 2, 1, rows]
        inverse = 1.0 / jnp.sum(total, axis=0, keepdims=True)
        delta = jnp.sum(delta, axis=0, keepdims=True) * inverse
        for rows in parts:
            weights = held[n % 2, 0, rows] * inverse
            wt[qi * 4 + head, rows] = weights.astype(jnp.bfloat16)
            ds[qi * 4 + head, rows] = (weights * (held[n % 2, 1, rows] - delta)).astype(
                jnp.bfloat16
            )
        if count < 4:
            rest = jnp.zeros(((4 - count) * BLOCK, BLOCK), jnp.bfloat16)
            wt[qi * 4 + head, count * BLOCK :] = rest
            ds[qi * 4 + head, count * BLOCK :] = rest

    def gradients(n):
        qi, chosen = items[n]
        for j, b in enumerate(chosen):
            rows = slice(j * BLOCK, (j + 1) * BLOCK)
            dk[b] += jnp.dot(
                ds[qi * 4 + head, rows], q[qi, :, lanes], preferred_element_type=jnp.float32
            )
            dv[b] += jnp.dot(
                wt[qi * 4 + head, rows], g[qi, :, lanes], preferred_element_type=jnp.float32
            )

    products(0)
    for n in range(unroll):
        if n + 1 < unroll:
            products(n + 1)
        if n > 0:
            gradients(n - 1)
        softmax(n)
    gradients(unroll - 1)


def attention_kernel(ring, unroll, lists, counts, q, g, k, v, wt, ds, dk, dv, held, own_lists, sem):
    place = Place(ring)
    copy = pltpu.make_async_copy(lists.at[pl.ds(place.head * 4, 4)], own_lists, sem)
    copy.start()

    @pl.loop(0, k.shape[0])
    def _(b):
        dk[b] = jnp.zeros((BLOCK, HEAD_WIDTH), jnp.float32)
        dv[b] = jnp.zeros((BLOCK, HEAD_WIDTH), jnp.float32)

    copy.wait()

    def picked(head, j, block):
        return own_lists[head, j, place.z * 4 + block]

    @pl.loop(0, 4)
    def _(head):
        used = counts[place.head * 4 + head]
        for count in range(1, 5):

            @pl.when(used == count)
            def _():
                @pl.loop(0, 8, step=unroll)
                def _(start):
                    attend(
                        count,
                        unroll,
                        ring,
                        head,
                        start,
                        q,
                        g,
                        k,
                        v,
                        wt,
                        ds,
                        dk,
                        dv,
                        picked,
                        held,
                    )


def attention(ring, lists, counts, qg, gg, kf, vf, unroll=8):
    items = jax.ShapeDtypeStruct((32, 4 * BLOCK, BLOCK), jnp.bfloat16)
    rows = jax.ShapeDtypeStruct(kf.shape, jnp.float32)
    return pl.pallas_call(
        functools.partial(attention_kernel, ring, unroll),
        out_shape=(items, items, rows, rows),
        in_specs=[ANY_SPEC, pl.BlockSpec(memory_space=pltpu.SMEM)] + [VMEM_SPEC] * 4,
        out_specs=(VMEM_SPEC,) * 4,
        scratch_shapes=[
            pltpu.VMEM((2, 2, 4 * BLOCK, BLOCK), jnp.float32),
            pltpu.SMEM((4, 4, lists.shape[2]), jnp.int32),
            pltpu.SemaphoreType.DMA,
        ],
        compiler_params=pltpu.CompilerParams(vmem_limit_bytes=32 << 20),
        name="attention",
    )(lists, counts, qg, gg, kf, vf)


def link_semaphores(ring):
    return [
        pltpu.SemaphoreType.DMA((4,)),
        pltpu.SemaphoreType.DMA((4, 3)),
        pltpu.SemaphoreType.DMA((4, 3)),
        pltpu.SemaphoreType.DMA((2, ring // 2, 8)),
        pltpu.SemaphoreType.DMA((2, ring // 2, 8)),
    ]


def local(queries, keys, values, grad_out, layout, counts):
    ring = lax.axis_size("context") // 2
    half = keys.shape[0]
    tokens = jax.ShapeDtypeStruct((4, queries.shape[0], GROUP_WIDTH), jnp.bfloat16)
    rows = jax.ShapeDtypeStruct((2 * ring, BLOCK, HEAD_WIDTH), jnp.bfloat16)
    outs = tuple(
        jax.ShapeDtypeStruct(x.shape, jnp.bfloat16) for x in (queries, queries, keys, values)
    )
    qg, gg, kf, vf, kt, vt = pl.pallas_call(
        functools.partial(gather_kernel, ring),
        out_shape=(tokens, tokens, rows, rows, rows, rows),
        in_specs=[HBM_SPEC] * 4,
        out_specs=(VMEM_SPEC,) * 6,
        scratch_shapes=link_semaphores(ring),
        compiler_params=pltpu.CompilerParams(
            collective_id=0, has_side_effects=True, vmem_limit_bytes=47 << 20
        ),
        name="gather",
    )(queries, grad_out, keys, values)
    shape = (8, BLOCK, GROUP_WIDTH)
    lists = layout.transpose(0, 2, 1)
    wt, ds, dk, dv = attention(ring, lists, counts, qg.reshape(shape), gg.reshape(shape), kf, vf)
    results = pl.pallas_call(
        functools.partial(scatter_kernel, ring),
        out_shape=outs,
        in_specs=[ANY_SPEC] + [VMEM_SPEC] * 6,
        out_specs=(VMEM_SPEC,) * 4,
        scratch_shapes=[
            pltpu.VMEM(tokens.shape, jnp.bfloat16),
            pltpu.VMEM(tokens.shape, jnp.bfloat16),
            pltpu.VMEM((2, 8, half, HEAD_WIDTH), jnp.bfloat16),
            pltpu.VMEM((2, 8, half, HEAD_WIDTH), jnp.bfloat16),
            pltpu.VMEM((2, ring // 2, 8, half, HEAD_WIDTH), jnp.bfloat16),
            pltpu.SMEM((4, 4, lists.shape[2]), jnp.int32),
            pltpu.SemaphoreType.DMA,
        ]
        + link_semaphores(ring),
        compiler_params=pltpu.CompilerParams(
            collective_id=1, has_side_effects=True, vmem_limit_bytes=24 << 20
        ),
        name="scatter",
    )(lists, wt, ds, kt, vt, dk, dv)
    return pl.pallas_call(
        output_kernel,
        out_shape=outs,
        in_specs=[ANY_SPEC] * 4,
        out_specs=(HBM_SPEC,) * 4,
        scratch_shapes=[pltpu.SemaphoreType.DMA((4,))],
        compiler_params=pltpu.CompilerParams(vmem_limit_bytes=1 << 20),
        name="output",
    )(*results)


def solution(mesh):
    placed = P(("dp", "context"), None)
    return jax.shard_map(
        local,
        mesh=mesh,
        in_specs=(placed, placed, placed, placed, P(), P()),
        out_specs=(placed,) * 4,
        check_vma=False,
    )
```

```python
import functools
import math

import jax
import jax.numpy as jnp
from jax import lax
from jax.experimental import pallas as pl
from jax.experimental.pallas import tpu as pltpu
from jax.sharding import PartitionSpec as P

QUERY_HEADS = 16
KEY_VALUE_HEADS = 4
HEAD_WIDTH = 128
BLOCK = 128
GROUP_WIDTH = 4 * HEAD_WIDTH
MESH = pl.DeviceIdType.MESH
VMEM_SPEC = pl.BlockSpec(memory_space=pltpu.VMEM)
ANY_SPEC = pl.BlockSpec(memory_space=pl.ANY)
HBM_SPEC = pl.BlockSpec(memory_space=pltpu.HBM)
SCALE = 1.0 / math.sqrt(HEAD_WIDTH)
SCALE_LOG2E = SCALE / math.log(2.0)
ROUTES = ((0, 0), (0, 1), (1, 0), (1, 1))


class Place:
    def __init__(self, ring):
        dp = lax.axis_index("dp")
        context = lax.axis_index("context")
        self.ring = ring
        self.dp = dp
        self.member = dp % 2
        self.core = context % 2
        self.z = context // 2
        self.head = self.member * 2 + self.core

    def partner(self, route, step=0):
        flip_member, flip_core = route
        member = 1 - self.member if flip_member else self.member
        core = 1 - self.core if flip_core else self.core
        z = (self.z + step + self.ring) % self.ring
        return member, core, member * 2 + core, (self.dp - self.member + member, z * 2 + core)

    def greet(self):
        barrier = pltpu.get_barrier_semaphore()
        others = [
            self.partner(route, step)[3] for step in (1, -1, 0) for route in ROUTES if step or any(route)
        ]
        for other in others:
            pl.semaphore_signal(barrier, inc=1, device_id=other, device_id_type=MESH)
        return barrier, len(others)


def columns(index, width):
    return pl.ds(pl.multiple_of(index * width, width), width)


def remote(source, landing, send_sem, recv_sem, device):
    return pltpu.make_async_remote_copy(
        src_ref=source,
        dst_ref=landing,
        send_sem=send_sem,
        recv_sem=recv_sem,
        device_id=device,
        device_id_type=MESH,
    )


SIGNS = (1, -1)
PIECES = [(t, i) for i in (2, 3, 1, 0) for t in range(2)]
BLOCKS = [(t, flip) for flip in range(2) for t in range(2)]


def gather_kernel(
    ring, q, g, k, v, qg, gg, kf, vf, kt, vt, own_sem, send_x, recv_x, send_z, recv_z
):
    place = Place(ring)
    barrier, expected = place.greet()
    pl.semaphore_wait(barrier, expected)
    half = k.shape[0]
    far = ring // 2

    def rows(buffer, route, z):
        member, core, _, _ = place.partner(route)
        return buffer.at[member * ring + z, columns(core, half), :]

    def chunk_z(way, chunk):
        return (place.z - SIGNS[way] * chunk + ring) % ring

    first, near = [], []
    for t, i in PIECES:
        piece = (k, v)[t].at[:, columns(place.partner(ROUTES[i])[2], HEAD_WIDTH)]
        landing = rows((kf, vf)[t], ROUTES[0], place.z)
        for way in range(2):
            first.append(
                remote(
                    piece,
                    landing,
                    send_z.at[way, 0, t * 4 + i],
                    recv_z.at[way, 0, t * 4 + i],
                    place.partner(ROUTES[i], SIGNS[way])[3],
                )
            )
            first[-1].start()
    for t, i in PIECES:
        piece = (k, v)[t].at[:, columns(place.partner(ROUTES[i])[2], HEAD_WIDTH)]
        landing = rows((kf, vf)[t], ROUTES[0], place.z)
        if i == 0:
            copy = pltpu.make_async_copy(piece, landing, own_sem.at[t])
        else:
            copy = remote(
                piece,
                landing,
                send_x.at[t, i - 1],
                recv_x.at[t, i - 1],
                place.partner(ROUTES[i])[3],
            )
        near.append((i, copy))
        copy.start()
    large = []
    for t, (source, target) in enumerate(((q, qg), (g, gg))):
        for i in (2, 3, 1, 0):
            _, _, head, device = place.partner(ROUTES[i])
            piece = source.at[:, columns(head, GROUP_WIDTH)]
            landing = target.at[place.head]
            if i == 0:
                copy = pltpu.make_async_copy(piece, landing, own_sem.at[2 + t])
            else:
                copy = remote(
                    piece, landing, send_x.at[2 + t, i - 1], recv_x.at[2 + t, i - 1], device
                )
            large.append(copy)
            copy.start()

    def block_of(flip, z):
        member = 1 - place.member if flip else place.member
        return member * ring + z

    def hop(way, chunk, slot, t, flip):
        block = (kf, vf)[t].at[block_of(flip, chunk_z(way, chunk))]
        return remote(
            block,
            block,
            send_z.at[way, slot, t * 2 + flip],
            recv_z.at[way, slot, t * 2 + flip],
            place.partner(ROUTES[0], SIGNS[way])[3],
        )

    def first_arrival(way, t, i):
        piece = rows((kf, vf)[t], ROUTES[i], chunk_z(way, 1))
        return remote(
            piece,
            piece,
            send_z.at[way, 0, t * 4 + i],
            recv_z.at[way, 0, t * 4 + i],
            place.partner(ROUTES[i], SIGNS[way])[3],
        )

    def turn(z):
        for member in range(2):
            block = member * ring + z
            kt[block] = kf[block].T
            vt[block] = vf[block].T

    for t, flip in BLOCKS:
        for way in range(2):
            for core in range(2):
                first_arrival(way, t, 2 * flip + core).wait_recv()
            hop(way, 1, 1, t, flip).start()
    for way in range(2):
        turn(chunk_z(way, 1))

    def forward(step, carry):
        for t, flip in BLOCKS:
            for way in range(2):
                hop(way, step, step - 1, t, flip).wait_recv()
                hop(way, step, step, t, flip).start()
        for way in range(2):
            turn(chunk_z(way, step))
        return carry

    lax.fori_loop(2, far - 1, forward, 0)
    for t, flip in BLOCKS:
        for way in range(2):
            hop(way, far - 1, far - 2, t, flip).wait_recv()
            if flip == way:
                hop(way, far - 1, far - 1, t, flip).start()
    for way in range(2):
        turn(chunk_z(way, far - 1))
    for i, copy in near:
        copy.wait() if i == 0 else copy.wait_recv()
    turn(place.z)
    for t, flip in BLOCKS:
        hop(flip, far, far - 1, t, flip).wait_recv()
    turn(chunk_z(0, far))

    def drain(step, carry):
        for t, flip in BLOCKS:
            for way in range(2):
                hop(way, step, step, t, flip).wait_send()
        return carry

    for copy in first:
        copy.wait_send()
    lax.fori_loop(1, far - 1, drain, 0)
    for t, flip in BLOCKS:
        hop(flip, far - 1, far - 1, t, flip).wait_send()
    for i, copy in near:
        if i > 0:
            copy.wait_send()
    for copy in large:
        copy.wait()


def scatter_kernel(
    ring,
    lists,
    wt,
    ds,
    kt,
    vt,
    dk,
    dv,
    att,
    dqo,
    dko,
    dvo,
    o,
    dq,
    first,
    own,
    landed,
    arrived,
    own_lists,
    list_sem,
    own_sem,
    send_x,
    recv_x,
    send_z,
    recv_z,
):
    place = Place(ring)
    barrier, expected = place.greet()
    list_copy = pltpu.make_async_copy(lists.at[pl.ds(place.head * 4, 4)], own_lists, list_sem)
    list_copy.start()
    half = dko.shape[0]
    far = ring // 2

    def partial(way, distance, t, flip):
        member = 1 - place.member if flip else place.member
        z = (place.z + SIGNS[way] * distance + ring) % ring
        return (dk, dv)[t].at[member * ring + z]

    def start_distance(way, flip):
        return far if flip == way else far - 1

    for t, flip in BLOCKS:
        for way in range(2):
            block = partial(way, start_distance(way, flip), t, flip)
            first[way, t * 2 + flip] = block[...].astype(jnp.bfloat16)
    pl.semaphore_wait(barrier, expected)

    def hop(source, way, slot, t, flip):
        return remote(
            source,
            landed.at[way, slot, t * 2 + flip],
            send_z.at[way, slot, t * 2 + flip],
            recv_z.at[way, slot, t * 2 + flip],
            place.partner(ROUTES[0], SIGNS[way])[3],
        )

    def last_hop(way, t, i):
        core = place.partner(ROUTES[i])[1]
        return remote(
            landed.at[way, 1, t * 2 + i // 2, columns(core, half), :],
            arrived.at[way, t * 4 + i],
            send_z.at[way, 0, t * 4 + i],
            recv_z.at[way, 0, t * 4 + i],
            place.partner(ROUTES[i], SIGNS[way])[3],
        )

    def pass_on(way, distance, t, flip, last=False):
        slot = landed.at[way, distance, t * 2 + flip]
        hop(slot, way, distance, t, flip).wait_recv()
        slot[...] = (slot[...].astype(jnp.float32) + partial(way, distance, t, flip)[...]).astype(
            jnp.bfloat16
        )
        if last:
            for core in range(2):
                last_hop(way, t, 2 * flip + core).start()
        else:
            hop(slot, way, distance - 1, t, flip).start()

    for t, flip in BLOCKS:
        for way in range(2):
            slot = start_distance(way, flip) - 1
            hop(first.at[way, t * 2 + flip], way, slot, t, flip).start()
    copies = []
    for t, i in PIECES:
        piece = t * 4 + i
        core = place.partner(ROUTES[i])[1]
        own[0, piece] = partial(0, 0, t, i // 2)[columns(core, half), :].astype(jnp.bfloat16)
        if i > 0:
            copies.append(
                remote(
                    own.at[0, piece],
                    own.at[1, piece],
                    send_x.at[2 + t, i - 1],
                    recv_x.at[2 + t, i - 1],
                    place.partner(ROUTES[i])[3],
                )
            )
            copies[-1].start()
    def finish(i):
        _, _, slot, device = place.partner(ROUTES[i])
        for block in range(2):
            qi = slot * 2 + block
            at = place.z * 4 + qi // 4 * (ring * 4) + qi % 4
            rows = slice(block * BLOCK, (block + 1) * BLOCK)
            for head in range(4):
                lanes = slice(head * HEAD_WIDTH, (head + 1) * HEAD_WIDTH)
                chosen = [own_lists[head, j, at] for j in range(4)]
                out = jnp.dot(
                    jnp.concatenate([vt[b] for b in chosen], 1),
                    wt[qi * 4 + head],
                    preferred_element_type=jnp.float32,
                )
                o[slot, rows, lanes] = out.T.astype(jnp.bfloat16)
                out = jnp.dot(
                    jnp.concatenate([kt[b] for b in chosen], 1),
                    ds[qi * 4 + head],
                    preferred_element_type=jnp.float32,
                )
                dq[slot, rows, lanes] = (out.T * SCALE).astype(jnp.bfloat16)
        for t, (source, target) in enumerate(((o, att), (dq, dqo))):
            landing = target.at[:, columns(place.head, GROUP_WIDTH)]
            if i == 0:
                copy = pltpu.make_async_copy(source.at[slot], landing, own_sem.at[t])
            else:
                copy = remote(
                    source.at[slot], landing, send_x.at[t, i - 1], recv_x.at[t, i - 1], device
                )
            copies.append(copy)
            copy.start()

    list_copy.wait()
    finish(2)
    for t, flip in BLOCKS:
        pass_on(flip, far - 1, t, flip)
    finish(3)
    for distance in (far - 2, far - 3):
        for t, flip in BLOCKS:
            for way in range(2):
                pass_on(way, distance, t, flip)
        finish(far - 1 - distance if distance == far - 2 else 0)

    def steps(n, carry):
        for t, flip in BLOCKS:
            for way in range(2):
                pass_on(way, far - 4 - n, t, flip)
        return carry

    lax.fori_loop(0, far - 5, steps, 0)
    for t, flip in reversed(BLOCKS):
        for way in range(2):
            pass_on(way, 1, t, flip, True)
    for copy in copies[:6]:
        copy.wait_recv()
    for t, i in reversed(PIECES):
        piece = t * 4 + i
        for way in range(2):
            last_hop(way, t, i).wait_recv()
        total = arrived[0, piece].astype(jnp.float32) + arrived[1, piece].astype(jnp.float32)
        total = total + own[1 if i > 0 else 0, piece].astype(jnp.float32)
        if t == 0:
            total = total * SCALE
        (dko, dvo)[t][:, columns(place.partner(ROUTES[i])[2], HEAD_WIDTH)] = total.astype(
            jnp.bfloat16
        )

    def drain(step, carry):
        for t, flip in BLOCKS:
            for way in range(2):
                hop(landed.at[way, step, t * 2 + flip], way, step, t, flip).wait_send()
        return carry

    lax.fori_loop(1, far - 1, drain, 0)
    for t, flip in BLOCKS:
        hop(landed.at[flip, far - 1, t * 2 + flip], flip, far - 1, t, flip).wait_send()
    for t, i in PIECES:
        for way in range(2):
            last_hop(way, t, i).wait_send()
    for n, copy in enumerate(copies):
        if n < 6:
            copy.wait_send()
        else:
            copy.wait()


def output_kernel(*refs):
    sources, targets, sems = refs[:4], refs[4:8], refs[8]
    copies = [
        pltpu.make_async_copy(source, target, sems.at[n])
        for n, (source, target) in enumerate(zip(sources, targets))
    ]
    for copy in copies:
        copy.start()
    for copy in copies:
        copy.wait()


def attend(count, unroll, z_blocks, head, start, q, g, k, v, wt, ds, dk, dv, picked, held):
    lanes = columns(head, HEAD_WIDTH)
    nt = (((1,), (1,)), ((), ()))
    items = []
    for u in range(unroll):
        qi = start + u
        block = qi // 4 * (z_blocks * 4) + qi % 4
        items.append((qi, [picked(head, j, block) for j in range(count)]))

    def products(n):
        qi, chosen = items[n]
        for j, b in enumerate(chosen):
            rows = slice(j * BLOCK, (j + 1) * BLOCK)
            held[n % 2, 0, rows] = lax.dot_general(
                k[b], q[qi, :, lanes], nt, preferred_element_type=jnp.float32
            )
            held[n % 2, 1, rows] = lax.dot_general(
                v[b], g[qi, :, lanes], nt, preferred_element_type=jnp.float32
            )

    def softmax(n):
        qi, chosen = items[n]
        parts = [slice(j * BLOCK, (j + 1) * BLOCK) for j in range(count)]
        peak = functools.reduce(jnp.maximum, [held[n % 2, 0, rows] for rows in parts])
        peak = jnp.max(peak, axis=0, keepdims=True)
        total = delta = 0.0
        for rows in parts:
            powers = jnp.exp2((held[n % 2, 0, rows] - peak) * SCALE_LOG2E)
            held[n % 2, 0, rows] = powers
            total = total + powers
            delta = delta + powers * held[n % 2, 1, rows]
        inverse = 1.0 / jnp.sum(total, axis=0, keepdims=True)
        delta = jnp.sum(delta, axis=0, keepdims=True) * inverse
        for rows in parts:
            weights = held[n % 2, 0, rows] * inverse
            wt[qi * 4 + head, rows] = weights.astype(jnp.bfloat16)
            ds[qi * 4 + head, rows] = (weights * (held[n % 2, 1, rows] - delta)).astype(
                jnp.bfloat16
            )
        if count < 4:
            rest = jnp.zeros(((4 - count) * BLOCK, BLOCK), jnp.bfloat16)
            wt[qi * 4 + head, count * BLOCK :] = rest
            ds[qi * 4 + head, count * BLOCK :] = rest

    def gradients(n):
        qi, chosen = items[n]
        for j, b in enumerate(chosen):
            rows = slice(j * BLOCK, (j + 1) * BLOCK)
            dk[b] += jnp.dot(
                ds[qi * 4 + head, rows], q[qi, :, lanes], preferred_element_type=jnp.float32
            )
            dv[b] += jnp.dot(
                wt[qi * 4 + head, rows], g[qi, :, lanes], preferred_element_type=jnp.float32
            )

    products(0)
    for n in range(unroll):
        if n + 1 < unroll:
            products(n + 1)
        if n > 0:
            gradients(n - 1)
        softmax(n)
    gradients(unroll - 1)


def attention_kernel(ring, unroll, lists, counts, q, g, k, v, wt, ds, dk, dv, held, own_lists, sem):
    place = Place(ring)
    copy = pltpu.make_async_copy(lists.at[pl.ds(place.head * 4, 4)], own_lists, sem)
    copy.start()

    @pl.loop(0, k.shape[0])
    def _(b):
        dk[b] = jnp.zeros((BLOCK, HEAD_WIDTH), jnp.float32)
        dv[b] = jnp.zeros((BLOCK, HEAD_WIDTH), jnp.float32)

    copy.wait()

    def picked(head, j, block):
        return own_lists[head, j, place.z * 4 + block]

    @pl.loop(0, 4)
    def _(head):
        used = counts[place.head * 4 + head]
        for count in range(1, 5):

            @pl.when(used == count)
            def _():
                @pl.loop(0, 8, step=unroll)
                def _(start):
                    attend(
                        count,
                        unroll,
                        ring,
                        head,
                        start,
                        q,
                        g,
                        k,
                        v,
                        wt,
                        ds,
                        dk,
                        dv,
                        picked,
                        held,
                    )


def attention(ring, lists, counts, qg, gg, kf, vf, unroll=8):
    items = jax.ShapeDtypeStruct((32, 4 * BLOCK, BLOCK), jnp.bfloat16)
    rows = jax.ShapeDtypeStruct(kf.shape, jnp.float32)
    return pl.pallas_call(
        functools.partial(attention_kernel, ring, unroll),
        out_shape=(items, items, rows, rows),
        in_specs=[ANY_SPEC, pl.BlockSpec(memory_space=pltpu.SMEM)] + [VMEM_SPEC] * 4,
        out_specs=(VMEM_SPEC,) * 4,
        scratch_shapes=[
            pltpu.VMEM((2, 2, 4 * BLOCK, BLOCK), jnp.float32),
            pltpu.SMEM((4, 4, lists.shape[2]), jnp.int32),
            pltpu.SemaphoreType.DMA,
        ],
        compiler_params=pltpu.CompilerParams(vmem_limit_bytes=32 << 20),
        name="attention",
    )(lists, counts, qg, gg, kf, vf)


def link_semaphores(ring):
    return [
        pltpu.SemaphoreType.DMA((4,)),
        pltpu.SemaphoreType.DMA((4, 3)),
        pltpu.SemaphoreType.DMA((4, 3)),
        pltpu.SemaphoreType.DMA((2, ring // 2, 8)),
        pltpu.SemaphoreType.DMA((2, ring // 2, 8)),
    ]


def local(queries, keys, values, grad_out, layout, counts):
    ring = lax.axis_size("context") // 2
    half = keys.shape[0]
    tokens = jax.ShapeDtypeStruct((4, queries.shape[0], GROUP_WIDTH), jnp.bfloat16)
    rows = jax.ShapeDtypeStruct((2 * ring, BLOCK, HEAD_WIDTH), jnp.bfloat16)
    outs = tuple(
        jax.ShapeDtypeStruct(x.shape, jnp.bfloat16) for x in (queries, queries, keys, values)
    )
    qg, gg, kf, vf, kt, vt = pl.pallas_call(
        functools.partial(gather_kernel, ring),
        out_shape=(tokens, tokens, rows, rows, rows, rows),
        in_specs=[HBM_SPEC] * 4,
        out_specs=(VMEM_SPEC,) * 6,
        scratch_shapes=link_semaphores(ring),
        compiler_params=pltpu.CompilerParams(
            collective_id=0, has_side_effects=True, vmem_limit_bytes=47 << 20
        ),
        name="gather",
    )(queries, grad_out, *(pltpu.with_memory_space_constraint(x, pltpu.HBM) for x in (keys, values)))
    shape = (8, BLOCK, GROUP_WIDTH)
    lists = layout.transpose(0, 2, 1)
    wt, ds, dk, dv = attention(ring, lists, counts, qg.reshape(shape), gg.reshape(shape), kf, vf)
    results = pl.pallas_call(
        functools.partial(scatter_kernel, ring),
        out_shape=outs,
        in_specs=[ANY_SPEC] + [VMEM_SPEC] * 6,
        out_specs=(VMEM_SPEC,) * 4,
        scratch_shapes=[
            pltpu.VMEM(tokens.shape, jnp.bfloat16),
            pltpu.VMEM(tokens.shape, jnp.bfloat16),
            pltpu.VMEM((2, 4, BLOCK, HEAD_WIDTH), jnp.bfloat16),
            pltpu.VMEM((2, 8, half, HEAD_WIDTH), jnp.bfloat16),
            pltpu.VMEM((2, ring // 2, 4, BLOCK, HEAD_WIDTH), jnp.bfloat16),
            pltpu.VMEM((2, 8, half, HEAD_WIDTH), jnp.bfloat16),
            pltpu.SMEM((4, 4, lists.shape[2]), jnp.int32),
            pltpu.SemaphoreType.DMA,
        ]
        + link_semaphores(ring),
        compiler_params=pltpu.CompilerParams(
            collective_id=1, has_side_effects=True, vmem_limit_bytes=24 << 20
        ),
        name="scatter",
    )(lists, wt, ds, kt, vt, dk, dv)
    return pl.pallas_call(
        output_kernel,
        out_shape=outs,
        in_specs=[ANY_SPEC] * 4,
        out_specs=(HBM_SPEC,) * 4,
        scratch_shapes=[pltpu.SemaphoreType.DMA((4,))],
        compiler_params=pltpu.CompilerParams(vmem_limit_bytes=1 << 20),
        name="output",
    )(*results)


def solution(mesh):
    placed = P(("dp", "context"), None)
    return jax.shard_map(
        local,
        mesh=mesh,
        in_specs=(placed, placed, placed, placed, P(), P()),
        out_specs=(placed,) * 4,
        check_vma=False,
    )
```

```python
import functools
import math

import jax
import jax.numpy as jnp
from jax import lax
from jax.experimental import pallas as pl
from jax.experimental.pallas import tpu as pltpu
from jax.sharding import PartitionSpec as P

QUERY_HEADS = 16
KEY_VALUE_HEADS = 4
HEAD_WIDTH = 128
BLOCK = 128
GROUP_WIDTH = 4 * HEAD_WIDTH
MESH = pl.DeviceIdType.MESH
VMEM_SPEC = pl.BlockSpec(memory_space=pltpu.VMEM)
ANY_SPEC = pl.BlockSpec(memory_space=pl.ANY)
HBM_SPEC = pl.BlockSpec(memory_space=pltpu.HBM)
SCALE = 1.0 / math.sqrt(HEAD_WIDTH)
SCALE_LOG2E = SCALE / math.log(2.0)
ROUTES = ((0, 0), (0, 1), (1, 0), (1, 1))


class Place:
    def __init__(self, ring):
        dp = lax.axis_index("dp")
        context = lax.axis_index("context")
        self.ring = ring
        self.dp = dp
        self.member = dp % 2
        self.core = context % 2
        self.z = context // 2
        self.head = self.member * 2 + self.core

    def partner(self, route, step=0):
        flip_member, flip_core = route
        member = 1 - self.member if flip_member else self.member
        core = 1 - self.core if flip_core else self.core
        z = (self.z + step + self.ring) % self.ring
        return member, core, member * 2 + core, (self.dp - self.member + member, z * 2 + core)

    def greet(self):
        barrier = pltpu.get_barrier_semaphore()
        others = [
            self.partner(route, step)[3] for step in (1, -1, 0) for route in ROUTES if step or any(route)
        ]
        for other in others:
            pl.semaphore_signal(barrier, inc=1, device_id=other, device_id_type=MESH)
        return barrier, len(others)


def columns(index, width):
    return pl.ds(pl.multiple_of(index * width, width), width)


def remote(source, landing, send_sem, recv_sem, device):
    return pltpu.make_async_remote_copy(
        src_ref=source,
        dst_ref=landing,
        send_sem=send_sem,
        recv_sem=recv_sem,
        device_id=device,
        device_id_type=MESH,
    )


SIGNS = (1, -1)
PIECES = [(t, i) for i in (2, 3, 1, 0) for t in range(2)]
BLOCKS = [(t, flip) for flip in range(2) for t in range(2)]


def gather_kernel(
    ring, q, g, k, v, qg, gg, kf, vf, kt, vt, own_sem, send_x, recv_x, send_z, recv_z
):
    place = Place(ring)
    barrier, expected = place.greet()
    pl.semaphore_wait(barrier, expected)
    half = k.shape[0]
    far = ring // 2

    def rows(buffer, route, z):
        member, core, _, _ = place.partner(route)
        return buffer.at[member * ring + z, columns(core, half), :]

    def chunk_z(way, chunk):
        return (place.z - SIGNS[way] * chunk + ring) % ring

    first, near = [], []
    for t, i in PIECES:
        piece = (k, v)[t].at[:, columns(place.partner(ROUTES[i])[2], HEAD_WIDTH)]
        landing = rows((kf, vf)[t], ROUTES[0], place.z)
        for way in range(2):
            first.append(
                remote(
                    piece,
                    landing,
                    send_z.at[way, 0, t * 4 + i],
                    recv_z.at[way, 0, t * 4 + i],
                    place.partner(ROUTES[i], SIGNS[way])[3],
                )
            )
            first[-1].start()
    for t, i in PIECES:
        piece = (k, v)[t].at[:, columns(place.partner(ROUTES[i])[2], HEAD_WIDTH)]
        landing = rows((kf, vf)[t], ROUTES[0], place.z)
        if i == 0:
            copy = pltpu.make_async_copy(piece, landing, own_sem.at[t])
        else:
            copy = remote(
                piece,
                landing,
                send_x.at[t, i - 1],
                recv_x.at[t, i - 1],
                place.partner(ROUTES[i])[3],
            )
        near.append((i, copy))
        copy.start()
    large = []
    for t, (source, target) in enumerate(((q, qg), (g, gg))):
        for i in (2, 3, 1, 0):
            _, _, head, device = place.partner(ROUTES[i])
            piece = source.at[:, columns(head, GROUP_WIDTH)]
            landing = target.at[place.head]
            if i == 0:
                copy = pltpu.make_async_copy(piece, landing, own_sem.at[2 + t])
            else:
                copy = remote(
                    piece, landing, send_x.at[2 + t, i - 1], recv_x.at[2 + t, i - 1], device
                )
            large.append(copy)
            copy.start()

    def block_of(flip, z):
        member = 1 - place.member if flip else place.member
        return member * ring + z

    def hop(way, chunk, slot, t, flip):
        block = (kf, vf)[t].at[block_of(flip, chunk_z(way, chunk))]
        return remote(
            block,
            block,
            send_z.at[way, slot, t * 2 + flip],
            recv_z.at[way, slot, t * 2 + flip],
            place.partner(ROUTES[0], SIGNS[way])[3],
        )

    def first_arrival(way, t, i):
        piece = rows((kf, vf)[t], ROUTES[i], chunk_z(way, 1))
        return remote(
            piece,
            piece,
            send_z.at[way, 0, t * 4 + i],
            recv_z.at[way, 0, t * 4 + i],
            place.partner(ROUTES[i], SIGNS[way])[3],
        )

    def turn(z):
        for member in range(2):
            block = member * ring + z
            kt[block] = kf[block].T
            vt[block] = vf[block].T

    for t, flip in BLOCKS:
        for way in range(2):
            for core in range(2):
                first_arrival(way, t, 2 * flip + core).wait_recv()
            hop(way, 1, 1, t, flip).start()
    for way in range(2):
        turn(chunk_z(way, 1))

    def forward(step, carry):
        for t, flip in BLOCKS:
            for way in range(2):
                hop(way, step, step - 1, t, flip).wait_recv()
                hop(way, step, step, t, flip).start()
        for way in range(2):
            turn(chunk_z(way, step))
        return carry

    lax.fori_loop(2, far - 1, forward, 0)
    for t, flip in BLOCKS:
        for way in range(2):
            hop(way, far - 1, far - 2, t, flip).wait_recv()
            if flip == way:
                hop(way, far - 1, far - 1, t, flip).start()
    for way in range(2):
        turn(chunk_z(way, far - 1))
    for i, copy in near:
        copy.wait() if i == 0 else copy.wait_recv()
    turn(place.z)
    for t, flip in BLOCKS:
        hop(flip, far, far - 1, t, flip).wait_recv()
    turn(chunk_z(0, far))

    def drain(step, carry):
        for t, flip in BLOCKS:
            for way in range(2):
                hop(way, step, step, t, flip).wait_send()
        return carry

    for copy in first:
        copy.wait_send()
    lax.fori_loop(1, far - 1, drain, 0)
    for t, flip in BLOCKS:
        hop(flip, far - 1, far - 1, t, flip).wait_send()
    for i, copy in near:
        if i > 0:
            copy.wait_send()
    for copy in large:
        copy.wait()


def scatter_kernel(
    ring,
    lists,
    wt,
    ds,
    kt,
    vt,
    dk,
    dv,
    att,
    dqo,
    dko,
    dvo,
    o,
    dq,
    first,
    own,
    landed,
    own_lists,
    list_sem,
    own_sem,
    send_x,
    recv_x,
    send_z,
    recv_z,
):
    place = Place(ring)
    barrier, expected = place.greet()
    list_copy = pltpu.make_async_copy(lists.at[pl.ds(place.head * 4, 4)], own_lists, list_sem)
    list_copy.start()
    half = dko.shape[0]
    far = ring // 2

    def partial(way, distance, t, i):
        member, core, _, _ = place.partner(ROUTES[i])
        z = (place.z + SIGNS[way] * distance + ring) % ring
        return (dk, dv)[t][member * ring + z, columns(core, half), :]

    def longer(way, i):
        return i % 2 == way

    for t, i in PIECES:
        for way in range(2):
            distance = far if longer(way, i) else far - 1
            first[way, t * 4 + i] = partial(way, distance, t, i).astype(jnp.bfloat16)
    pl.semaphore_wait(barrier, expected)

    def hop(source, way, slot, t, i, last=False):
        return remote(
            source,
            landed.at[way, slot, t * 4 + i],
            send_z.at[way, slot, t * 4 + i],
            recv_z.at[way, slot, t * 4 + i],
            place.partner(ROUTES[i if last else 0], SIGNS[way])[3],
        )

    def pass_on(way, distance, t, i, last=False):
        slot = landed.at[way, distance, t * 4 + i]
        hop(slot, way, distance, t, i).wait_recv()
        slot[...] = (slot[...].astype(jnp.float32) + partial(way, distance, t, i)).astype(
            jnp.bfloat16
        )
        hop(slot, way, distance - 1, t, i, last).start()

    for t, i in PIECES:
        for way in range(2):
            distance = far if longer(way, i) else far - 1
            hop(first.at[way, t * 4 + i], way, distance - 1, t, i).start()
    copies = []
    for t, i in PIECES:
        piece = t * 4 + i
        own[0, piece] = partial(0, 0, t, i).astype(jnp.bfloat16)
        if i > 0:
            copies.append(
                remote(
                    own.at[0, piece],
                    own.at[1, piece],
                    send_x.at[2 + t, i - 1],
                    recv_x.at[2 + t, i - 1],
                    place.partner(ROUTES[i])[3],
                )
            )
            copies[-1].start()
    def finish(i):
        _, _, slot, device = place.partner(ROUTES[i])
        for block in range(2):
            qi = slot * 2 + block
            at = place.z * 4 + qi // 4 * (ring * 4) + qi % 4
            rows = slice(block * BLOCK, (block + 1) * BLOCK)
            for head in range(4):
                lanes = slice(head * HEAD_WIDTH, (head + 1) * HEAD_WIDTH)
                chosen = [own_lists[head, j, at] for j in range(4)]
                out = jnp.dot(
                    jnp.concatenate([vt[b] for b in chosen], 1),
                    wt[qi * 4 + head],
                    preferred_element_type=jnp.float32,
                )
                o[slot, rows, lanes] = out.T.astype(jnp.bfloat16)
                out = jnp.dot(
                    jnp.concatenate([kt[b] for b in chosen], 1),
                    ds[qi * 4 + head],
                    preferred_element_type=jnp.float32,
                )
                dq[slot, rows, lanes] = (out.T * SCALE).astype(jnp.bfloat16)
        for t, (source, target) in enumerate(((o, att), (dq, dqo))):
            landing = target.at[:, columns(place.head, GROUP_WIDTH)]
            if i == 0:
                copy = pltpu.make_async_copy(source.at[slot], landing, own_sem.at[t])
            else:
                copy = remote(
                    source.at[slot], landing, send_x.at[t, i - 1], recv_x.at[t, i - 1], device
                )
            copies.append(copy)
            copy.start()

    list_copy.wait()
    finish(2)
    for t, i in PIECES:
        pass_on(i % 2, far - 1, t, i)
    finish(3)
    for distance in (far - 2, far - 3):
        for t, i in PIECES:
            for way in range(2):
                pass_on(way, distance, t, i)
        finish(far - 1 - distance if distance == far - 2 else 0)

    def steps(n, carry):
        for t, i in PIECES:
            for way in range(2):
                pass_on(way, far - 4 - n, t, i)
        return carry

    lax.fori_loop(0, far - 5, steps, 0)
    for t, i in PIECES:
        for way in range(2):
            pass_on(way, 1, t, i, True)
    for copy in copies[:6]:
        copy.wait_recv()
    for t, i in reversed(PIECES):
        piece = t * 4 + i
        for way in range(2):
            hop(landed.at[way, 0, piece], way, 0, t, i, True).wait_recv()
        total = landed[0, 0, piece].astype(jnp.float32) + landed[1, 0, piece].astype(jnp.float32)
        total = total + own[1 if i > 0 else 0, piece].astype(jnp.float32)
        if t == 0:
            total = total * SCALE
        (dko, dvo)[t][:, columns(place.partner(ROUTES[i])[2], HEAD_WIDTH)] = total.astype(
            jnp.bfloat16
        )

    def drain(step, carry):
        for t, i in PIECES:
            for way in range(2):
                hop(landed.at[way, step, t * 4 + i], way, step, t, i).wait_send()
        return carry

    lax.fori_loop(1, far - 1, drain, 0)
    for t, i in PIECES:
        for way in range(2):
            hop(landed.at[way, 0, t * 4 + i], way, 0, t, i, True).wait_send()
        hop(landed.at[i % 2, far - 1, t * 4 + i], i % 2, far - 1, t, i).wait_send()
    for n, copy in enumerate(copies):
        if n < 6:
            copy.wait_send()
        else:
            copy.wait()


def output_kernel(*refs):
    sources, targets, sems = refs[:4], refs[4:8], refs[8]
    copies = [
        pltpu.make_async_copy(source, target, sems.at[n])
        for n, (source, target) in enumerate(zip(sources, targets))
    ]
    for copy in copies:
        copy.start()
    for copy in copies:
        copy.wait()


def attend(count, unroll, z_blocks, head, start, q, g, k, v, wt, ds, dk, dv, picked, held):
    lanes = columns(head, HEAD_WIDTH)
    nt = (((1,), (1,)), ((), ()))
    items = []
    for u in range(unroll):
        qi = start + u
        block = qi // 4 * (z_blocks * 4) + qi % 4
        items.append((qi, [picked(head, j, block) for j in range(count)]))

    def products(n):
        qi, chosen = items[n]
        for t, (source, other) in enumerate(((k, q), (v, g))):
            held[n % 2, t, : count * BLOCK] = lax.dot_general(
                jnp.concatenate([source[b] for b in chosen], 0),
                other[qi, :, lanes],
                nt,
                preferred_element_type=jnp.float32,
            )

    def softmax(n):
        qi, chosen = items[n]
        parts = [slice(j * BLOCK, (j + 1) * BLOCK) for j in range(count)]
        peak = functools.reduce(jnp.maximum, [held[n % 2, 0, rows] for rows in parts])
        peak = jnp.max(peak, axis=0, keepdims=True)
        total = delta = 0.0
        for rows in parts:
            powers = jnp.exp2((held[n % 2, 0, rows] - peak) * SCALE_LOG2E)
            held[n % 2, 0, rows] = powers
            total = total + powers
            delta = delta + powers * held[n % 2, 1, rows]
        inverse = 1.0 / jnp.sum(total, axis=0, keepdims=True)
        delta = jnp.sum(delta, axis=0, keepdims=True) * inverse
        for rows in parts:
            weights = held[n % 2, 0, rows] * inverse
            wt[qi * 4 + head, rows] = weights.astype(jnp.bfloat16)
            ds[qi * 4 + head, rows] = (weights * (held[n % 2, 1, rows] - delta)).astype(
                jnp.bfloat16
            )
        if count < 4:
            rest = jnp.zeros(((4 - count) * BLOCK, BLOCK), jnp.bfloat16)
            wt[qi * 4 + head, count * BLOCK :] = rest
            ds[qi * 4 + head, count * BLOCK :] = rest

    def gradients(n):
        qi, chosen = items[n]
        for source, other, target in ((ds, q, dk), (wt, g, dv)):
            product = jnp.dot(
                source[qi * 4 + head, : count * BLOCK],
                other[qi, :, lanes],
                preferred_element_type=jnp.float32,
            )
            for j, b in enumerate(chosen):
                target[b] += product[j * BLOCK : (j + 1) * BLOCK]

    products(0)
    for n in range(unroll):
        if n + 1 < unroll:
            products(n + 1)
        if n > 0:
            gradients(n - 1)
        softmax(n)
    gradients(unroll - 1)


def attention_kernel(ring, unroll, lists, counts, q, g, k, v, wt, ds, dk, dv, held, own_lists, used_counts, sems):
    place = Place(ring)
    copies = [
        pltpu.make_async_copy(lists.at[pl.ds(place.head * 4, 4)], own_lists, sems.at[0]),
        pltpu.make_async_copy(counts, used_counts, sems.at[1]),
    ]
    for copy in copies:
        copy.start()

    @pl.loop(0, k.shape[0])
    def _(b):
        dk[b] = jnp.zeros((BLOCK, HEAD_WIDTH), jnp.float32)
        dv[b] = jnp.zeros((BLOCK, HEAD_WIDTH), jnp.float32)

    for copy in copies:
        copy.wait()

    def picked(head, j, block):
        return own_lists[head, j, place.z * 4 + block]

    @pl.loop(0, 4)
    def _(head):
        used = used_counts[place.head * 4 + head]
        for count in range(1, 5):

            @pl.when(used == count)
            def _():
                @pl.loop(0, 8, step=unroll)
                def _(start):
                    attend(
                        count,
                        unroll,
                        ring,
                        head,
                        start,
                        q,
                        g,
                        k,
                        v,
                        wt,
                        ds,
                        dk,
                        dv,
                        picked,
                        held,
                    )


def attention(ring, lists, counts, qg, gg, kf, vf, unroll=8):
    items = jax.ShapeDtypeStruct((32, 4 * BLOCK, BLOCK), jnp.bfloat16)
    rows = jax.ShapeDtypeStruct(kf.shape, jnp.float32)
    return pl.pallas_call(
        functools.partial(attention_kernel, ring, unroll),
        out_shape=(items, items, rows, rows),
        in_specs=[HBM_SPEC, HBM_SPEC] + [VMEM_SPEC] * 4,
        out_specs=(VMEM_SPEC,) * 4,
        scratch_shapes=[
            pltpu.VMEM((2, 2, 4 * BLOCK, BLOCK), jnp.float32),
            pltpu.SMEM((4, 4, lists.shape[2]), jnp.int32),
            pltpu.SMEM(counts.shape, jnp.int32),
            pltpu.SemaphoreType.DMA((2,)),
        ],
        compiler_params=pltpu.CompilerParams(vmem_limit_bytes=32 << 20),
        name="attention",
    )(lists, counts, qg, gg, kf, vf)


def link_semaphores(ring):
    return [
        pltpu.SemaphoreType.DMA((4,)),
        pltpu.SemaphoreType.DMA((4, 3)),
        pltpu.SemaphoreType.DMA((4, 3)),
        pltpu.SemaphoreType.DMA((2, ring // 2, 8)),
        pltpu.SemaphoreType.DMA((2, ring // 2, 8)),
    ]


def in_hbm(x):
    return pltpu.with_memory_space_constraint(x, pltpu.HBM)


def local(queries, keys, values, grad_out, layout, counts):
    ring = lax.axis_size("context") // 2
    half = keys.shape[0]
    tokens = jax.ShapeDtypeStruct((4, queries.shape[0], GROUP_WIDTH), jnp.bfloat16)
    rows = jax.ShapeDtypeStruct((2 * ring, BLOCK, HEAD_WIDTH), jnp.bfloat16)
    outs = tuple(
        jax.ShapeDtypeStruct(x.shape, jnp.bfloat16) for x in (queries, queries, keys, values)
    )
    qg, gg, kf, vf, kt, vt = pl.pallas_call(
        functools.partial(gather_kernel, ring),
        out_shape=(tokens, tokens, rows, rows, rows, rows),
        in_specs=[HBM_SPEC] * 4,
        out_specs=(VMEM_SPEC,) * 6,
        scratch_shapes=link_semaphores(ring),
        compiler_params=pltpu.CompilerParams(
            collective_id=0, has_side_effects=True, vmem_limit_bytes=47 << 20
        ),
        name="gather",
    )(queries, grad_out, in_hbm(keys), in_hbm(values))
    shape = (8, BLOCK, GROUP_WIDTH)
    lists = in_hbm(layout.transpose(0, 2, 1))
    counts = in_hbm(counts)
    wt, ds, dk, dv = attention(ring, lists, counts, qg.reshape(shape), gg.reshape(shape), kf, vf)
    results = pl.pallas_call(
        functools.partial(scatter_kernel, ring),
        out_shape=outs,
        in_specs=[HBM_SPEC] + [VMEM_SPEC] * 6,
        out_specs=(VMEM_SPEC,) * 4,
        scratch_shapes=[
            pltpu.VMEM(tokens.shape, jnp.bfloat16),
            pltpu.VMEM(tokens.shape, jnp.bfloat16),
            pltpu.VMEM((2, 8, half, HEAD_WIDTH), jnp.bfloat16),
            pltpu.VMEM((2, 8, half, HEAD_WIDTH), jnp.bfloat16),
            pltpu.VMEM((2, ring // 2, 8, half, HEAD_WIDTH), jnp.bfloat16),
            pltpu.SMEM((4, 4, lists.shape[2]), jnp.int32),
            pltpu.SemaphoreType.DMA,
        ]
        + link_semaphores(ring),
        compiler_params=pltpu.CompilerParams(
            collective_id=1, has_side_effects=True, vmem_limit_bytes=24 << 20
        ),
        name="scatter",
    )(lists, wt, ds, kt, vt, dk, dv)
    return pl.pallas_call(
        output_kernel,
        out_shape=outs,
        in_specs=[ANY_SPEC] * 4,
        out_specs=(HBM_SPEC,) * 4,
        scratch_shapes=[pltpu.SemaphoreType.DMA((4,))],
        compiler_params=pltpu.CompilerParams(vmem_limit_bytes=1 << 20),
        name="output",
    )(*results)


def solution(mesh):
    placed = P(("dp", "context"), None)
    return jax.shard_map(
        local,
        mesh=mesh,
        in_specs=(placed, placed, placed, placed, P(), P()),
        out_specs=(placed,) * 4,
        check_vma=False,
    )
```

```python
import functools
import math

import jax
import jax.numpy as jnp
from jax import lax
from jax.experimental import pallas as pl
from jax.experimental.pallas import tpu as pltpu
from jax.sharding import PartitionSpec as P

QUERY_HEADS = 16
KEY_VALUE_HEADS = 4
HEAD_WIDTH = 128
BLOCK = 128
GROUP_WIDTH = 4 * HEAD_WIDTH
MESH = pl.DeviceIdType.MESH
VMEM_SPEC = pl.BlockSpec(memory_space=pltpu.VMEM)
ANY_SPEC = pl.BlockSpec(memory_space=pl.ANY)
HBM_SPEC = pl.BlockSpec(memory_space=pltpu.HBM)
SCALE = 1.0 / math.sqrt(HEAD_WIDTH)
SCALE_LOG2E = SCALE / math.log(2.0)
ROUTES = ((0, 0), (0, 1), (1, 0), (1, 1))


class Place:
    def __init__(self, ring):
        dp = lax.axis_index("dp")
        context = lax.axis_index("context")
        self.ring = ring
        self.dp = dp
        self.member = dp % 2
        self.core = context % 2
        self.z = context // 2
        self.head = self.member * 2 + self.core

    def partner(self, route, step=0):
        flip_member, flip_core = route
        member = 1 - self.member if flip_member else self.member
        core = 1 - self.core if flip_core else self.core
        z = (self.z + step + self.ring) % self.ring
        return member, core, member * 2 + core, (self.dp - self.member + member, z * 2 + core)

    def greet(self):
        barrier = pltpu.get_barrier_semaphore()
        others = [
            self.partner(route, step)[3] for step in (1, -1, 0) for route in ROUTES if step or any(route)
        ]
        for other in others:
            pl.semaphore_signal(barrier, inc=1, device_id=other, device_id_type=MESH)
        return barrier, len(others)


def columns(index, width):
    return pl.ds(pl.multiple_of(index * width, width), width)


def remote(source, landing, send_sem, recv_sem, device):
    return pltpu.make_async_remote_copy(
        src_ref=source,
        dst_ref=landing,
        send_sem=send_sem,
        recv_sem=recv_sem,
        device_id=device,
        device_id_type=MESH,
    )


SIGNS = (1, -1)
PIECES = [(t, i) for i in (2, 3, 1, 0) for t in range(2)]
BLOCKS = [(t, flip) for flip in range(2) for t in range(2)]


def gather_kernel(
    ring, q, g, k, v, qg, gg, kf, vf, kt, vt, own_sem, send_x, recv_x, send_z, recv_z
):
    place = Place(ring)
    barrier, expected = place.greet()
    pl.semaphore_wait(barrier, expected)
    half = k.shape[0]
    far = ring // 2

    def rows(buffer, route, z):
        member, core, _, _ = place.partner(route)
        return buffer.at[member * ring + z, columns(core, half), :]

    def chunk_z(way, chunk):
        return (place.z - SIGNS[way] * chunk + ring) % ring

    first, near = [], []
    for t, i in PIECES:
        piece = (k, v)[t].at[:, columns(place.partner(ROUTES[i])[2], HEAD_WIDTH)]
        landing = rows((kf, vf)[t], ROUTES[0], place.z)
        for way in range(2):
            first.append(
                remote(
                    piece,
                    landing,
                    send_z.at[way, 0, t * 4 + i],
                    recv_z.at[way, 0, t * 4 + i],
                    place.partner(ROUTES[i], SIGNS[way])[3],
                )
            )
            first[-1].start()
    for t, i in PIECES:
        piece = (k, v)[t].at[:, columns(place.partner(ROUTES[i])[2], HEAD_WIDTH)]
        landing = rows((kf, vf)[t], ROUTES[0], place.z)
        if i == 0:
            copy = pltpu.make_async_copy(piece, landing, own_sem.at[t])
        else:
            copy = remote(
                piece,
                landing,
                send_x.at[t, i - 1],
                recv_x.at[t, i - 1],
                place.partner(ROUTES[i])[3],
            )
        near.append((i, copy))
        copy.start()
    large = []
    for t, (source, target) in enumerate(((q, qg), (g, gg))):
        for i in (2, 3, 1, 0):
            _, _, head, device = place.partner(ROUTES[i])
            piece = source.at[:, columns(head, GROUP_WIDTH)]
            landing = target.at[place.head]
            if i == 0:
                copy = pltpu.make_async_copy(piece, landing, own_sem.at[2 + t])
            else:
                copy = remote(
                    piece, landing, send_x.at[2 + t, i - 1], recv_x.at[2 + t, i - 1], device
                )
            large.append(copy)
            copy.start()

    def block_of(flip, z):
        member = 1 - place.member if flip else place.member
        return member * ring + z

    def hop(way, chunk, slot, t, flip):
        block = (kf, vf)[t].at[block_of(flip, chunk_z(way, chunk))]
        return remote(
            block,
            block,
            send_z.at[way, slot, t * 2 + flip],
            recv_z.at[way, slot, t * 2 + flip],
            place.partner(ROUTES[0], SIGNS[way])[3],
        )

    def first_arrival(way, t, i):
        piece = rows((kf, vf)[t], ROUTES[i], chunk_z(way, 1))
        return remote(
            piece,
            piece,
            send_z.at[way, 0, t * 4 + i],
            recv_z.at[way, 0, t * 4 + i],
            place.partner(ROUTES[i], SIGNS[way])[3],
        )

    def turn(z):
        for member in range(2):
            block = member * ring + z
            kt[block] = kf[block].T
            vt[block] = vf[block].T

    for t, flip in BLOCKS:
        for way in range(2):
            for core in range(2):
                first_arrival(way, t, 2 * flip + core).wait_recv()
            hop(way, 1, 1, t, flip).start()
    for way in range(2):
        turn(chunk_z(way, 1))

    def forward(step, carry):
        for t, flip in BLOCKS:
            for way in range(2):
                hop(way, step, step - 1, t, flip).wait_recv()
                hop(way, step, step, t, flip).start()
        for way in range(2):
            turn(chunk_z(way, step))
        return carry

    for step in range(2, far - 1):
        forward(step, 0)
    for t, flip in BLOCKS:
        for way in range(2):
            hop(way, far - 1, far - 2, t, flip).wait_recv()
            if flip == way:
                hop(way, far - 1, far - 1, t, flip).start()
    for way in range(2):
        turn(chunk_z(way, far - 1))
    for i, copy in near:
        copy.wait() if i == 0 else copy.wait_recv()
    turn(place.z)
    for t, flip in BLOCKS:
        hop(flip, far, far - 1, t, flip).wait_recv()
    turn(chunk_z(0, far))

    def drain(step, carry):
        for t, flip in BLOCKS:
            for way in range(2):
                hop(way, step, step, t, flip).wait_send()
        return carry

    for copy in first:
        copy.wait_send()
    lax.fori_loop(1, far - 1, drain, 0)
    for t, flip in BLOCKS:
        hop(flip, far - 1, far - 1, t, flip).wait_send()
    for i, copy in near:
        if i > 0:
            copy.wait_send()
    for copy in large:
        copy.wait()


def scatter_kernel(
    ring,
    lists,
    wt,
    ds,
    kt,
    vt,
    dk,
    dv,
    att,
    dqo,
    dko,
    dvo,
    o,
    dq,
    first,
    own,
    landed,
    own_lists,
    list_sem,
    own_sem,
    send_x,
    recv_x,
    send_z,
    recv_z,
):
    place = Place(ring)
    barrier, expected = place.greet()
    list_copy = pltpu.make_async_copy(lists.at[pl.ds(place.head * 4, 4)], own_lists, list_sem)
    list_copy.start()
    half = dko.shape[0]
    far = ring // 2

    def partial(way, distance, t, i):
        member, core, _, _ = place.partner(ROUTES[i])
        z = (place.z + SIGNS[way] * distance + ring) % ring
        return (dk, dv)[t][member * ring + z, columns(core, half), :]

    def longer(way, i):
        return i % 2 == way

    for t, i in PIECES:
        for way in range(2):
            distance = far if longer(way, i) else far - 1
            first[way, t * 4 + i] = partial(way, distance, t, i).astype(jnp.bfloat16)
    pl.semaphore_wait(barrier, expected)

    def hop(source, way, slot, t, i, last=False):
        return remote(
            source,
            landed.at[way, slot, t * 4 + i],
            send_z.at[way, slot, t * 4 + i],
            recv_z.at[way, slot, t * 4 + i],
            place.partner(ROUTES[i if last else 0], SIGNS[way])[3],
        )

    def pass_on(way, distance, t, i, last=False):
        slot = landed.at[way, distance, t * 4 + i]
        hop(slot, way, distance, t, i).wait_recv()
        slot[...] = (slot[...].astype(jnp.float32) + partial(way, distance, t, i)).astype(
            jnp.bfloat16
        )
        hop(slot, way, distance - 1, t, i, last).start()

    for t, i in PIECES:
        for way in range(2):
            distance = far if longer(way, i) else far - 1
            hop(first.at[way, t * 4 + i], way, distance - 1, t, i).start()
    copies = []
    for t, i in PIECES:
        piece = t * 4 + i
        own[0, piece] = partial(0, 0, t, i).astype(jnp.bfloat16)
        if i > 0:
            copies.append(
                remote(
                    own.at[0, piece],
                    own.at[1, piece],
                    send_x.at[2 + t, i - 1],
                    recv_x.at[2 + t, i - 1],
                    place.partner(ROUTES[i])[3],
                )
            )
            copies[-1].start()
    def finish(i):
        _, _, slot, device = place.partner(ROUTES[i])
        for block in range(2):
            qi = slot * 2 + block
            at = place.z * 4 + qi // 4 * (ring * 4) + qi % 4
            rows = slice(block * BLOCK, (block + 1) * BLOCK)
            for head in range(4):
                lanes = slice(head * HEAD_WIDTH, (head + 1) * HEAD_WIDTH)
                chosen = [own_lists[head, j, at] for j in range(4)]
                out = jnp.dot(
                    jnp.concatenate([vt[b] for b in chosen], 1),
                    wt[qi * 4 + head],
                    preferred_element_type=jnp.float32,
                )
                o[slot, rows, lanes] = out.T.astype(jnp.bfloat16)
                out = jnp.dot(
                    jnp.concatenate([kt[b] for b in chosen], 1),
                    ds[qi * 4 + head],
                    preferred_element_type=jnp.float32,
                )
                dq[slot, rows, lanes] = (out.T * SCALE).astype(jnp.bfloat16)
        for t, (source, target) in enumerate(((o, att), (dq, dqo))):
            landing = target.at[:, columns(place.head, GROUP_WIDTH)]
            if i == 0:
                copy = pltpu.make_async_copy(source.at[slot], landing, own_sem.at[t])
            else:
                copy = remote(
                    source.at[slot], landing, send_x.at[t, i - 1], recv_x.at[t, i - 1], device
                )
            copies.append(copy)
            copy.start()

    list_copy.wait()
    finish(2)
    for t, i in PIECES:
        pass_on(i % 2, far - 1, t, i)
    finish(3)
    for distance in (far - 2, far - 3):
        for t, i in PIECES:
            for way in range(2):
                pass_on(way, distance, t, i)
        finish(far - 1 - distance if distance == far - 2 else 0)

    def steps(n, carry):
        for t, i in PIECES:
            for way in range(2):
                pass_on(way, far - 4 - n, t, i)
        return carry

    for n in range(far - 5):
        steps(n, 0)
    for t, i in PIECES:
        for way in range(2):
            pass_on(way, 1, t, i, True)
    for copy in copies[:6]:
        copy.wait_recv()
    for t, i in reversed(PIECES):
        piece = t * 4 + i
        for way in range(2):
            hop(landed.at[way, 0, piece], way, 0, t, i, True).wait_recv()
        total = landed[0, 0, piece].astype(jnp.float32) + landed[1, 0, piece].astype(jnp.float32)
        total = total + own[1 if i > 0 else 0, piece].astype(jnp.float32)
        if t == 0:
            total = total * SCALE
        (dko, dvo)[t][:, columns(place.partner(ROUTES[i])[2], HEAD_WIDTH)] = total.astype(
            jnp.bfloat16
        )

    def drain(step, carry):
        for t, i in PIECES:
            for way in range(2):
                hop(landed.at[way, step, t * 4 + i], way, step, t, i).wait_send()
        return carry

    lax.fori_loop(1, far - 1, drain, 0)
    for t, i in PIECES:
        for way in range(2):
            hop(landed.at[way, 0, t * 4 + i], way, 0, t, i, True).wait_send()
        hop(landed.at[i % 2, far - 1, t * 4 + i], i % 2, far - 1, t, i).wait_send()
    for n, copy in enumerate(copies):
        if n < 6:
            copy.wait_send()
        else:
            copy.wait()


def output_kernel(*refs):
    sources, targets, sems = refs[:4], refs[4:8], refs[8]
    copies = [
        pltpu.make_async_copy(source, target, sems.at[n])
        for n, (source, target) in enumerate(zip(sources, targets))
    ]
    for copy in copies:
        copy.start()
    for copy in copies:
        copy.wait()


def attend(count, unroll, z_blocks, head, start, q, g, k, v, wt, ds, dk, dv, picked, held):
    lanes = columns(head, HEAD_WIDTH)
    nt = (((1,), (1,)), ((), ()))
    items = []
    for u in range(unroll):
        qi = start + u
        block = qi // 4 * (z_blocks * 4) + qi % 4
        items.append((qi, [picked(head, j, block) for j in range(count)]))

    def products(n):
        qi, chosen = items[n]
        for t, (source, other) in enumerate(((k, q), (v, g))):
            held[n % 2, t, : count * BLOCK] = lax.dot_general(
                jnp.concatenate([source[b] for b in chosen], 0),
                other[qi, :, lanes],
                nt,
                preferred_element_type=jnp.float32,
            )

    def softmax(n):
        qi, chosen = items[n]
        parts = [slice(j * BLOCK, (j + 1) * BLOCK) for j in range(count)]
        peak = functools.reduce(jnp.maximum, [held[n % 2, 0, rows] for rows in parts])
        peak = jnp.max(peak, axis=0, keepdims=True)
        total = delta = 0.0
        for rows in parts:
            powers = jnp.exp2((held[n % 2, 0, rows] - peak) * SCALE_LOG2E)
            held[n % 2, 0, rows] = powers
            total = total + powers
            delta = delta + powers * held[n % 2, 1, rows]
        inverse = 1.0 / jnp.sum(total, axis=0, keepdims=True)
        delta = jnp.sum(delta, axis=0, keepdims=True) * inverse
        for rows in parts:
            weights = held[n % 2, 0, rows] * inverse
            wt[qi * 4 + head, rows] = weights.astype(jnp.bfloat16)
            ds[qi * 4 + head, rows] = (weights * (held[n % 2, 1, rows] - delta)).astype(
                jnp.bfloat16
            )
        if count < 4:
            rest = jnp.zeros(((4 - count) * BLOCK, BLOCK), jnp.bfloat16)
            wt[qi * 4 + head, count * BLOCK :] = rest
            ds[qi * 4 + head, count * BLOCK :] = rest

    def gradients(n):
        qi, chosen = items[n]
        for source, other, target in ((ds, q, dk), (wt, g, dv)):
            product = jnp.dot(
                source[qi * 4 + head, : count * BLOCK],
                other[qi, :, lanes],
                preferred_element_type=jnp.float32,
            )
            for j, b in enumerate(chosen):
                target[b] += product[j * BLOCK : (j + 1) * BLOCK]

    products(0)
    for n in range(unroll):
        if n + 1 < unroll:
            products(n + 1)
        if n > 0:
            gradients(n - 1)
        softmax(n)
    gradients(unroll - 1)


def attention_kernel(ring, unroll, lists, counts, q, g, k, v, wt, ds, dk, dv, held, own_lists, used_counts, sems):
    place = Place(ring)
    copies = [
        pltpu.make_async_copy(lists.at[pl.ds(place.head * 4, 4)], own_lists, sems.at[0]),
        pltpu.make_async_copy(counts, used_counts, sems.at[1]),
    ]
    for copy in copies:
        copy.start()

    @pl.loop(0, k.shape[0])
    def _(b):
        dk[b] = jnp.zeros((BLOCK, HEAD_WIDTH), jnp.float32)
        dv[b] = jnp.zeros((BLOCK, HEAD_WIDTH), jnp.float32)

    for copy in copies:
        copy.wait()

    def picked(head, j, block):
        return own_lists[head, j, place.z * 4 + block]

    @pl.loop(0, 4)
    def _(head):
        used = used_counts[place.head * 4 + head]
        for count in range(1, 5):

            @pl.when(used == count)
            def _():
                @pl.loop(0, 8, step=unroll)
                def _(start):
                    attend(
                        count,
                        unroll,
                        ring,
                        head,
                        start,
                        q,
                        g,
                        k,
                        v,
                        wt,
                        ds,
                        dk,
                        dv,
                        picked,
                        held,
                    )


def attention(ring, lists, counts, qg, gg, kf, vf, unroll=8):
    items = jax.ShapeDtypeStruct((32, 4 * BLOCK, BLOCK), jnp.bfloat16)
    rows = jax.ShapeDtypeStruct(kf.shape, jnp.float32)
    return pl.pallas_call(
        functools.partial(attention_kernel, ring, unroll),
        out_shape=(items, items, rows, rows),
        in_specs=[HBM_SPEC, HBM_SPEC] + [VMEM_SPEC] * 4,
        out_specs=(VMEM_SPEC,) * 4,
        scratch_shapes=[
            pltpu.VMEM((2, 2, 4 * BLOCK, BLOCK), jnp.float32),
            pltpu.SMEM((4, 4, lists.shape[2]), jnp.int32),
            pltpu.SMEM(counts.shape, jnp.int32),
            pltpu.SemaphoreType.DMA((2,)),
        ],
        compiler_params=pltpu.CompilerParams(vmem_limit_bytes=32 << 20),
        name="attention",
    )(lists, counts, qg, gg, kf, vf)


def link_semaphores(ring):
    return [
        pltpu.SemaphoreType.DMA((4,)),
        pltpu.SemaphoreType.DMA((4, 3)),
        pltpu.SemaphoreType.DMA((4, 3)),
        pltpu.SemaphoreType.DMA((2, ring // 2, 8)),
        pltpu.SemaphoreType.DMA((2, ring // 2, 8)),
    ]


def in_hbm(x):
    return pltpu.with_memory_space_constraint(x, pltpu.HBM)


def local(queries, keys, values, grad_out, layout, counts):
    ring = lax.axis_size("context") // 2
    half = keys.shape[0]
    tokens = jax.ShapeDtypeStruct((4, queries.shape[0], GROUP_WIDTH), jnp.bfloat16)
    rows = jax.ShapeDtypeStruct((2 * ring, BLOCK, HEAD_WIDTH), jnp.bfloat16)
    outs = tuple(
        jax.ShapeDtypeStruct(x.shape, jnp.bfloat16) for x in (queries, queries, keys, values)
    )
    qg, gg, kf, vf, kt, vt = pl.pallas_call(
        functools.partial(gather_kernel, ring),
        out_shape=(tokens, tokens, rows, rows, rows, rows),
        in_specs=[HBM_SPEC] * 4,
        out_specs=(VMEM_SPEC,) * 6,
        scratch_shapes=link_semaphores(ring),
        compiler_params=pltpu.CompilerParams(
            collective_id=0, has_side_effects=True, vmem_limit_bytes=47 << 20
        ),
        name="gather",
    )(queries, grad_out, in_hbm(keys), in_hbm(values))
    shape = (8, BLOCK, GROUP_WIDTH)
    lists = in_hbm(layout.transpose(0, 2, 1))
    counts = in_hbm(counts)
    wt, ds, dk, dv = attention(ring, lists, counts, qg.reshape(shape), gg.reshape(shape), kf, vf)
    results = pl.pallas_call(
        functools.partial(scatter_kernel, ring),
        out_shape=outs,
        in_specs=[HBM_SPEC] + [VMEM_SPEC] * 6,
        out_specs=(VMEM_SPEC,) * 4,
        scratch_shapes=[
            pltpu.VMEM(tokens.shape, jnp.bfloat16),
            pltpu.VMEM(tokens.shape, jnp.bfloat16),
            pltpu.VMEM((2, 8, half, HEAD_WIDTH), jnp.bfloat16),
            pltpu.VMEM((2, 8, half, HEAD_WIDTH), jnp.bfloat16),
            pltpu.VMEM((2, ring // 2, 8, half, HEAD_WIDTH), jnp.bfloat16),
            pltpu.SMEM((4, 4, lists.shape[2]), jnp.int32),
            pltpu.SemaphoreType.DMA,
        ]
        + link_semaphores(ring),
        compiler_params=pltpu.CompilerParams(
            collective_id=1, has_side_effects=True, vmem_limit_bytes=24 << 20
        ),
        name="scatter",
    )(lists, wt, ds, kt, vt, dk, dv)
    return pl.pallas_call(
        output_kernel,
        out_shape=outs,
        in_specs=[ANY_SPEC] * 4,
        out_specs=(HBM_SPEC,) * 4,
        scratch_shapes=[pltpu.SemaphoreType.DMA((4,))],
        compiler_params=pltpu.CompilerParams(vmem_limit_bytes=1 << 20),
        name="output",
    )(*results)


def solution(mesh):
    placed = P(("dp", "context"), None)
    return jax.shard_map(
        local,
        mesh=mesh,
        in_specs=(placed, placed, placed, placed, P(), P()),
        out_specs=(placed,) * 4,
        check_vma=False,
    )
```
